256 devices in a mesh: panel: 2 (over core), ang: 32 (over z, x), rad: 4 (over y).
Axes of the slice: x: 4, y: 4, z: 8, core: 2. Of those that a mesh axis runs over, the one named last changes fastest.
Arguments:
- density: float32 [2, 8, 512, 512], P('panel', 'rad', 'ang'), may hold values from 1 to 2
- momentum: float32 [2, 3, 8, 512, 512], P('panel', None, 'rad', 'ang'), may hold values from -2.5 to 2.5
- magnetic: float32 [2, 3, 8, 512, 512], P('panel', None, 'rad', 'ang'), may hold values from -2.5 to 2.5
- partner_device: int32 [2, 1024, 1], P('panel', 'ang'), may hold values from 0 to 31; in each aligned block of 32 rows (0 to 31, 32 to 63, ..., all dimensions but the last counted through in order) at most 2 rows name the same one
- partner_phi: int32 [2, 1024], P('panel', 'ang'), may hold values from 0 to 14
- partner_theta: int32 [2, 1024], P('panel', 'ang'), may hold values from 0 to 510
- partner_weight: float32 [2, 1024, 4], P('panel', 'ang'), may hold values from 0 to 1, as said below
- border_turn: float32 [2, 1024], P('panel', 'ang'), may hold values from -3.140625 to 3.140625
Outputs:
- density_next: float32 [2, 8, 512, 512], P('panel', 'rad', 'ang')
- momentum_next: float32 [2, 3, 8, 512, 512], P('panel', None, 'rad', 'ang')
- magnetic_next: float32 [2, 3, 8, 512, 512], P('panel', None, 'rad', 'ang')
The draws below stay inside these ranges and needn't reach their ends.
Inputs may be any that keep to these rules, and one draw needn't show every extreme that they name: `partner_device`: within the 32 table rows of one device (aligned blocks), at most 2 rows name the same source device. `partner_weight`: each row's weights are (1-u)(1-v), (1-u)v, u(1-v), uv for some u, v in [0, 1].
All inputs are finite; a program needn't handle non-finite values.
Results may differ from the reference program's by a relative error of at most 0.00005.
Values sent between devices are 32-bit elements; how exact they have to be, the bound alone decides.
No kernel may reach another device: no remote copies, remote signals or barrier semaphores. Data moves between devices by JAX's collectives and lax.ppermute only.
A program may use at most 64 MiB of HBM per device.

```python
import math
import jax
import jax.numpy as jnp
import numpy as np

CP = 16
NT = 512
PANELS = 2
NR = 8
NP = 512
BORDER = 32
ANG_ROWS = 1024
MOST = 2
N_ANG = 32


def draw_partner_weight(key, part):
    first_key, second_key = jax.random.split(jax.random.fold_in(key, 17))
    along_phi = jax.random.uniform(first_key, (PANELS, ANG_ROWS), jnp.float32)
    along_theta = jax.random.uniform(second_key, (PANELS, ANG_ROWS), jnp.float32)
    return jnp.stack([(1.0 - along_phi) * (1.0 - along_theta), (1.0 - along_phi) * along_theta, along_phi * (1.0 - along_theta), along_phi * along_theta], axis=-1)


def with_ends(values, rng, least, high):
    index_at = [jax.random.randint(jax.random.fold_in(rng, axis), (), 0, length) for axis, length in enumerate(values.shape)]
    main_axis = values.shape.index(max(values.shape))
    next_to = index_at[:main_axis] + [(index_at[main_axis] + 1) % values.shape[main_axis]] + index_at[main_axis + 1:]
    return values.at[tuple(index_at)].set(least).at[tuple(next_to)].set(high)


def steps_of(key, dims, cuts, low, top_value):
    loudness = 1.0
    for axis_at, parts in cuts:
        steps = jax.random.uniform(jax.random.fold_in(jax.random.fold_in(key, 6), axis_at), (parts,), jnp.float32, low / len(cuts), top_value / len(cuts))
        loudness = loudness * jnp.repeat(jnp.exp(steps), dims[axis_at] // parts).reshape((-1,) + (1,) * (len(dims) - 1 - axis_at))
    return loudness


def shared_out(own_key, own, number, rows, amount, top, limit, skew):
    sequence = jax.random.permutation(own_key, amount)
    crowded, ordinary = portions_of(amount, rows * top, limit, skew, True), portions_of(amount, rows * top, limit, skew, False)
    places = jnp.arange(amount)

    def named(sizes, rotation):
        used = int((sizes > 0).sum())
        fixed = max(1, used // 4)
        passed = fixed + (places - fixed + rotation * (used - fixed)) % max(1, amount - fixed)
        return jnp.zeros((amount,), jnp.int32).at[sequence[jnp.where(places < fixed, places, passed)]].set(jnp.asarray(sizes, jnp.int32))

    sizes = jnp.where(number % 4 == 0, named(crowded, number // 4), named(ordinary, number - number // 4 - 1))
    mixed = jax.random.permutation(jax.random.fold_in(own, 3), amount)
    donor, receiver = mixed[0:amount // 2 * 2:2], mixed[1:amount // 2 * 2:2]
    slack = jnp.minimum(sizes[donor] - 1, limit - sizes[receiver]) // 2
    slack = jnp.where((donor == sequence[0]) | (receiver == sequence[0]) | (sizes[receiver] == 0), 0, jnp.maximum(slack, 0))
    passed = jax.random.randint(jax.random.fold_in(own, 4), (amount // 2,), 0, 1 << 20) % (slack + 1)
    sizes = sizes.at[donor].add(-passed).at[receiver].add(passed)
    members = jnp.searchsorted(jnp.cumsum(sizes), jnp.arange(rows * top), side="right").astype(jnp.int32)
    listing = members.reshape(top, rows).T
    listing = listing[jax.random.permutation(jax.random.fold_in(own, 1), rows)]
    rotation = jax.random.randint(jax.random.fold_in(own, 2), (rows, 1), 0, top)
    return jnp.take_along_axis(listing, (jnp.arange(top)[None, :] + rotation) % top, axis=1)


def portions_of(count, total, bound, slope, full):
    weights = [(1 << 20) // math.isqrt(standing ** slope) + 1 for standing in range(1, count + 1)]
    largest = bound if full else min(bound, max(-(-total // count), total * weights[0] // sum(weights)))
    least = 1 if total - largest >= count - 1 else 0
    holding, spare = [largest] + [least] * (count - 1), total - largest - least * (count - 1)
    while spare > 0:
        candidates = [i for i in range(1, count) if holding[i] < largest] or [i for i in range(1, count) if holding[i] < bound]
        whole, remaining = sum([weights[i] for i in candidates]), spare
        for i in candidates:
            more = min(bound - holding[i], max(1, remaining * weights[i] // whole), spare)
            holding[i] = holding[i] + more
            spare = spare - more
    return np.array(holding)


def normal_values(stream_key, shape, scale, limit, cuts=(), kind=jnp.bfloat16):
    values = scale * jax.random.normal(stream_key, shape, jnp.float32)
    if cuts:
        values = values * steps_of(stream_key, shape, cuts, -0.22, 0.18)
    return jnp.clip(values, -limit, limit).astype(kind)


def setup_inputs(seed: int = 0) -> dict:
    keys = jax.random.split(jax.random.key(seed), 9)
    density = jnp.clip(1.0 + 1.0 * jax.random.uniform(keys[0], (PANELS, NR, NP, NT), jnp.float32) ** steps_of(keys[0], (PANELS, NR, NP, NT), ((0, 2), (1, 4), (2, 32)), -0.2, 0.2), 1.0, 2.0)
    momentum = normal_values(keys[1], (PANELS, 3, NR, NP, NT), 0.3, 2.5, ((0, 2), (2, 4), (3, 32)), jnp.float32)
    magnetic = normal_values(keys[2], (PANELS, 3, NR, NP, NT), 0.4, 2.5, ((0, 2), (2, 4), (3, 32)), jnp.float32)
    partner_device_keys = jax.random.split(jax.random.fold_in(keys[3], 1), PANELS * ANG_ROWS // BORDER)
    partner_device_turns = jax.random.permutation(jax.random.fold_in(keys[3], 3), PANELS * ANG_ROWS // BORDER)
    partner_device = jax.vmap(lambda own, number: shared_out(jax.random.fold_in(keys[3], 2), own, number, BORDER, N_ANG, 1, MOST, 2))(partner_device_keys, partner_device_turns).reshape((PANELS, ANG_ROWS, 1))
    partner_phi = with_ends(jax.random.randint(keys[4], (PANELS, ANG_ROWS), 0, CP - 1), jax.random.fold_in(keys[4], 1), 0, (CP - 1) - 1).astype(jnp.int32)
    partner_theta = with_ends(jax.random.randint(keys[5], (PANELS, ANG_ROWS), 0, NT - 1), jax.random.fold_in(keys[5], 1), 0, (NT - 1) - 1).astype(jnp.int32)
    partner_weight = draw_partner_weight(jax.random.fold_in(keys[8], 71), 0)
    border_turn = jnp.clip(jax.random.uniform(keys[7], (PANELS, ANG_ROWS), jnp.float32, -3.140625, 3.140625), -3.140625, 3.140625)
    return dict(density=density, momentum=momentum, magnetic=magnetic, partner_device=partner_device, partner_phi=partner_phi, partner_theta=partner_theta, partner_weight=partner_weight, border_turn=border_turn)


time_step = 0.15
sound_sq = 1.0
viscosity = 0.1
resistivity = 0.1
r_inner = 0.35
corner_steps = ((0, 0), (0, 1), (1, 0), (1, 1))


def field_of(block, index):
    return block[..., index, :, :, :]


def fluxes(block, direction):
    mass_field = field_of(block, 0)
    moment = [field_of(block, 1 + component) for component in range(3)]
    magnet = [field_of(block, 4 + component) for component in range(3)]
    velocity = [moment[component] / mass_field for component in range(3)]
    pressure = sound_sq * mass_field + 0.5 * (magnet[0] * magnet[0] + magnet[1] * magnet[1] + magnet[2] * magnet[2])
    pieces = [moment[direction]]
    for component in range(3):
        flux_term = moment[component] * velocity[direction] - magnet[component] * magnet[direction]
        if component == direction:
            flux_term = flux_term + pressure
        pieces.append(flux_term)
    for component in range(3):
        pieces.append(velocity[direction] * magnet[component] - magnet[direction] * velocity[component])
    return jnp.stack(pieces, axis=-4)


def tendency(current, radial, polar, azimuth, half_t, half_p, sq_t, sq_p):
    flux_r = fluxes(radial, 0)
    flux_t = fluxes(polar, 1)
    flux_p = fluxes(azimuth, 2)
    divergence = (flux_r[..., 2:, :, :] - flux_r[..., :-2, :, :]) * 0.5
    divergence = divergence + (flux_t[..., 2:] - flux_t[..., :-2]) * half_t
    divergence = divergence + (flux_p[..., :, 2:, :] - flux_p[..., :, :-2, :]) * half_p
    laplace_sum = radial[..., 2:, :, :] - 2.0 * current + radial[..., :-2, :, :]
    laplace_sum = laplace_sum + (polar[..., 2:] - 2.0 * current + polar[..., :-2]) * sq_t
    laplace_sum = laplace_sum + (azimuth[..., :, 2:, :] - 2.0 * current + azimuth[..., :, :-2, :]) * sq_p
    mixing = jnp.array([0.0, viscosity, viscosity, viscosity, resistivity, resistivity, resistivity], jnp.float32).reshape(7, 1, 1, 1)
    return mixing * laplace_sum - divergence


def turn_frame(ghost, cosine, sine):
    pieces = [ghost[0], ghost[1]]
    pieces.append(cosine * ghost[2] + sine * ghost[3])
    pieces.append(cosine * ghost[3] - sine * ghost[2])
    pieces.append(ghost[4])
    pieces.append(cosine * ghost[5] + sine * ghost[6])
    pieces.append(cosine * ghost[6] - sine * ghost[5])
    return jnp.stack(pieces, axis=0)


def reference(density, momentum, magnetic, partner_device, partner_phi, partner_theta, partner_weight, border_turn):
    fields_now = jnp.concatenate([density[:, None], momentum, magnetic], axis=1)
    radius = r_inner + (jnp.arange(NR).astype(jnp.float32) + 0.5) * ((1.0 - r_inner) / NR)
    colatitude = math.pi / 4 + (jnp.arange(NT).astype(jnp.float32) + 0.5) * (math.pi / 2 / NT)
    inv_radius = (1.0 / radius).reshape(NR, 1, 1)
    inv_both = inv_radius / jnp.sin(colatitude)
    half_t = 0.5 * inv_radius
    half_p = 0.5 * inv_both
    sq_t = inv_radius * inv_radius
    sq_p = inv_both * inv_both
    mirror = jnp.array([1.0, -1.0, -1.0, -1.0, 1.0, 1.0, 1.0], jnp.float32).reshape(7, 1, 1, 1)
    phi_start = partner_device[..., 0] * CP + partner_phi

    def overset(current):
        lowers = []
        uppers = []
        for panel_side in range(2):
            source_grid = current[1 - panel_side]
            phi_base = phi_start[panel_side]
            theta_base = partner_theta[panel_side]
            weights = partner_weight[panel_side]
            values = [source_grid[:, :, phi_base + step_phi, theta_base + step_theta] for step_phi, step_theta in corner_steps]
            ghost = weights[:, 0] * values[0] + weights[:, 1] * values[1]
            ghost = ghost + weights[:, 2] * values[2]
            ghost = ghost + weights[:, 3] * values[3]
            angle = border_turn[panel_side]
            ghost = turn_frame(ghost, jnp.cos(angle), jnp.sin(angle))
            ghost = ghost.reshape(7, NR, N_ANG, 2, CP)
            lowers.append(ghost[:, :, :, 0, :].reshape(7, NR, NP))
            uppers.append(ghost[:, :, :, 1, :].reshape(7, NR, NP))
        return jnp.stack(lowers, axis=0), jnp.stack(uppers, axis=0)

    def evaluate(current):
        radial = jnp.concatenate([mirror * current[:, :, :1], current, mirror * current[:, :, -1:]], axis=2)
        azimuth = jnp.concatenate([mirror * current[:, :, :, :1], current, mirror * current[:, :, :, -1:]], axis=3)
        lower_t, upper_t = overset(current)
        polar = jnp.concatenate([lower_t[..., None], current, upper_t[..., None]], axis=4)
        return tendency(current, radial, polar, azimuth, half_t, half_p, sq_t, sq_p)

    slope_one = evaluate(fields_now)
    slope_two = evaluate(fields_now + (0.5 * time_step) * slope_one)
    slope_three = evaluate(fields_now + (0.5 * time_step) * slope_two)
    slope_four = evaluate(fields_now + time_step * slope_three)
    updated = fields_now + (time_step / 6.0) * (slope_one + 2.0 * slope_two + 2.0 * slope_three + slope_four)
    return updated[:, 0], updated[:, 1:4], updated[:, 4:7]
```

```python
import math

import jax
import jax.numpy as jnp
import numpy as np
from jax import lax
from jax.experimental import pallas as pl
from jax.experimental.pallas import tpu as pltpu
from jax.sharding import PartitionSpec as P

time_step = 0.15
diffusion = 0.1
r_inner = 0.35
NF = 7
MIRROR = (1.0, -1.0, -1.0, -1.0, 1.0, 1.0, 1.0)
INTERPRET = False
SLOT = 16
HIGHEST = lax.Precision.HIGHEST


def iota(shape, dim):
    return lax.broadcasted_iota(jnp.int32, shape, dim)


def derived(cells):
    inverse = 1.0 / cells[0]
    speed = [cells[1 + c] * inverse for c in range(3)]
    pressure = cells[0] + 0.5 * (
        cells[4] * cells[4] + cells[5] * cells[5] + cells[6] * cells[6]
    )
    return speed, pressure


def flux_along(cells, speed, pressure, d):
    moment, magnet = cells[1:4], cells[4:7]
    out = [moment[d]]
    for c in range(3):
        term = moment[c] * speed[d] - magnet[c] * magnet[d]
        out.append(term + pressure if c == d else term)
    for c in range(3):
        out.append(None if c == d else speed[d] * magnet[c] - magnet[d] * speed[c])
    return out


def upper_part(flux, cell, half, spread):
    if cell is None:
        return half * flux
    if flux is None:
        return -(spread * cell)
    return half * flux - spread * cell


def lower_part(flux, cell, half, spread):
    if cell is None:
        return half * flux
    if flux is None:
        return spread * cell
    return half * flux + spread * cell


def place(rad, n_rad, level, rows_r):
    value = None
    for at in range(n_rad):
        radius = r_inner + (at * rows_r + level + 0.5) * ((1.0 - r_inner) / (rows_r * n_rad))
        item = jnp.float32(1.0 / radius)
        value = item if value is None else jnp.where(rad == at, item, value)
    return value


def answer_into(msg_ref, low, high, corner, rowmask):
    rows_p = rowmask.shape[0]
    parts = []
    for level in (low, high):
        product = jnp.dot(level, corner, precision=HIGHEST, preferred_element_type=jnp.float32)
        picked = product.reshape(NF, rows_p, 128) * rowmask[None]
        parts.append(jnp.sum(picked, axis=1))
        parts.append(jnp.zeros((1, 128), jnp.float32))
    both = jnp.concatenate(parts, axis=0)
    both = both + pltpu.roll(both, 64, axis=1)
    turned = both.T
    lanes = jnp.concatenate([turned, jnp.zeros((128, 128 - SLOT), jnp.float32)], axis=1)
    lane = iota((32, 128), 1)
    message = jnp.where(lane < SLOT, lanes[0:32], pltpu.roll(lanes[32:64], SLOT, axis=1))
    msg_ref[...] = message.reshape(msg_ref.shape)


def send_rows(first_ref, last_ref, level, f, value):
    first_ref[f, level : level + 1, :] = value[0:1, :]
    last_ref[f, level : level + 1, :] = value[value.shape[0] - 1 :, :]


def open_kernel(
    density, momentum, magnetic, device, phi, theta, weight, turn, cos_in, sin_in,
    low_ref, high_ref, first_ref, last_ref, ask_ref, table_ref,
):
    for level, ref in ((0, low_ref), (1, high_ref)):
        for f in range(NF):
            if f == 0:
                value = density[0, level]
            elif f < 4:
                value = momentum[0, f - 1, level]
            else:
                value = magnetic[0, f - 4, level]
            ref[f] = value
            send_rows(first_ref, last_ref, level, f, value)
    rows = device.shape[1]
    one, two = iota((rows, rows), 0), iota((rows, rows), 1)
    eye = one == two
    dev_col = device[0]
    dev_row = jnp.sum(jnp.where(eye, jnp.broadcast_to(dev_col, (rows, rows)), 0), axis=0, keepdims=True)
    same = dev_col == dev_row
    rank_row = jnp.sum(jnp.where(same & (one < two), 1, 0), axis=0, keepdims=True)
    rank_col = jnp.sum(jnp.where(same & (two < one), 1, 0), axis=1, keepdims=True)

    def column(row):
        return jnp.sum(jnp.where(eye, jnp.broadcast_to(row, (rows, rows)), 0.0), axis=1, keepdims=True)

    phi_col = column(phi[...].astype(jnp.float32))
    theta_col = column(theta[...].astype(jnp.float32))
    weights = weight[0]
    lane = iota((rows, 128), 1)
    items = [phi_col, theta_col] + [weights[:, c : c + 1] for c in range(4)]
    record = jnp.zeros((rows, 128), jnp.float32)
    for at, item in enumerate(items):
        record = jnp.where(lane == at, item, record)
    asked = jnp.zeros((rows, 128), jnp.float32)
    for slot in range(2):
        placing = jnp.where((one == dev_row) & (rank_row == slot), 1.0, 0.0)
        moved = record if slot == 0 else pltpu.roll(record, 8, axis=1)
        asked = asked + jnp.dot(placing, moved, precision=HIGHEST, preferred_element_type=jnp.float32)
    ask_ref[...] = asked.reshape(ask_ref.shape)
    picks = jnp.where(((lane & 31) == dev_col) & ((lane >> 5) == rank_col) & (lane < 64), 1.0, 0.0)
    cosine = column(cos_in[...])
    sine = column(sin_in[...])
    picks = jnp.where(lane == 64, cosine, picks)
    table_ref[...] = jnp.where(lane == 65, sine, picks)


def asked_kernel(asked_ref, low_ref, high_ref, corner_ref, mask_ref, msg_ref):
    asked = asked_ref[...].reshape(32, 128)
    lane, sub = iota((32, 128), 1), iota((32, 128), 0)

    def row_of(at):
        total = jnp.zeros((32, 128), jnp.float32)
        for part in range(4):
            slot = part & 1
            col = asked[:, slot * 8 + at[part >> 1] : slot * 8 + at[part >> 1] + 1]
            total = jnp.where(lane == sub + 32 * part, col, total)
        return jnp.sum(total, axis=0, keepdims=True)

    phi_row = row_of((0, 0)).astype(jnp.int32)
    theta_row = row_of((1, 1)).astype(jnp.int32)
    near = row_of((2, 4))
    far = row_of((3, 5))
    cell = iota((corner_ref.shape[0], 128), 0)
    corner = jnp.where(cell == theta_row, near, jnp.where(cell == theta_row + 1, far, 0.0))
    corner_ref[...] = corner
    rows_p = mask_ref.shape[0]
    wanted = phi_row + jnp.where(iota((1, 128), 1) < 64, 0, 1)
    mask = jnp.where(iota((rows_p, 128), 0) == wanted, 1.0, 0.0)
    mask_ref[...] = mask
    rows_t = low_ref.shape[2]
    low = low_ref[...].reshape(NF * rows_p, rows_t)
    high = high_ref[...].reshape(NF * rows_p, rows_t)
    answer_into(msg_ref, low, high, corner, mask)


def stage_kernel(stage, n_rad, n_ang, *refs):
    last = stage == 4
    (flags, sines, low0, high0, below, above, before, after, reply, table) = refs[:10]
    refs = refs[10:]
    if stage == 1:
        low, high = low0, high0
    else:
        low, high, acc_low, acc_high = refs[:4]
        refs = refs[4:]
    if last:
        density_out, momentum_out, magnetic_out = refs[:3]
        refs = refs[3:]
    else:
        corner, rowmask = refs[:2]
        low_out, high_out, acc_low_out, acc_high_out, first_out, last_out, msg_out = refs[2:9]
        refs = refs[9:]
    slope, up, down = refs
    rad, ang = flags[0], flags[1]
    rows_p, rows_t = low.shape[1:]
    invs = [place(rad, n_rad, level, 2) for level in range(2)]

    got = reply[...].reshape(32, 128)
    picks = table[...]
    ghost = jnp.dot(picks[:, 0:32], got, precision=HIGHEST, preferred_element_type=jnp.float32)
    second = jnp.dot(picks[:, 32:64], got, precision=HIGHEST, preferred_element_type=jnp.float32)
    ghost = ghost + pltpu.roll(second, 128 - SLOT, axis=1)
    cosine, sine = picks[:, 64:65], picks[:, 65:66]
    lane = iota((32, 128), 1) & 7
    is_t = (lane == 2) | (lane == 5)
    is_p = (lane == 3) | (lane == 6)
    turned_t = cosine * ghost + sine * pltpu.roll(ghost, 127, axis=1)
    turned_p = cosine * ghost - sine * pltpu.roll(ghost, 1, axis=1)
    ghost = jnp.where(is_t, turned_t, jnp.where(is_p, turned_p, ghost))

    sine_row = sines[...]
    rim = []
    for f in range(NF):
        own = [low[f, 0:1, :], high[f, 0:1, :], low[f, rows_p - 1 :, :], high[f, rows_p - 1 :, :]]
        own = [MIRROR[f] * item for item in own]
        start = jnp.where(ang == 0, jnp.concatenate(own[:2], axis=0), before[f])
        end = jnp.where(ang == n_ang - 1, jnp.concatenate(own[2:], axis=0), after[f])
        rim.append(jnp.concatenate([start, end, start, end], axis=0))
    rim_row = iota((8, rows_t), 0) & 1
    rim_inv = jnp.where(rim_row == 0, invs[0], invs[1]) * sine_row
    speed, pressure = derived(rim)
    flux = flux_along(rim, speed, pressure, 2)
    rim_half, rim_spread = 0.5 * rim_inv, diffusion * rim_inv * rim_inv
    rim_low = [lower_part(flux[f], rim[f] if f else None, rim_half, rim_spread) for f in range(NF)]
    rim_high = [upper_part(flux[f], rim[f] if f else None, rim_half, rim_spread) for f in range(NF)]

    half_row = iota((8, 128), 1) < 64
    for tile in range(rows_p // 8):
        rows = slice(8 * tile, 8 * tile + 8)
        for level in range(2):
            mine, other = (low, high) if level == 0 else (high, low)
            far, wall = (below, rad == 0) if level == 0 else (above, rad == n_rad - 1)
            cells = [mine[f, rows, :] for f in range(NF)]
            sums = []
            outer = [jnp.where(wall, MIRROR[f] * cells[f], far[f, rows, :]) for f in range(NF)]
            speed, pressure = derived(outer)
            flux = flux_along(outer, speed, pressure, 0)
            part = lower_part if level == 0 else upper_part
            for f in range(NF):
                sums.append(part(flux[f], outer[f] if f else None, 0.5, diffusion))
            inner = [other[f, rows, :] for f in range(NF)]
            speed, pressure = derived(inner)
            flux = flux_along(inner, speed, pressure, 0)
            part = upper_part if level == 0 else lower_part
            for f in range(NF):
                item = part(flux[f], inner[f] if f else None, 0.5, diffusion)
                sums[f] = sums[f] - item if level == 0 else item - sums[f]
            speed, pressure = derived(cells)
            inv = invs[level]
            inv_sine = inv * sine_row
            half, spread = 0.5 * inv_sine, diffusion * inv_sine * inv_sine
            flux = flux_along(cells, speed, pressure, 2)
            for f in range(NF):
                cell = cells[f] if f else None
                down[level, f, rows, :] = lower_part(flux[f], cell, half, spread)
                up[level, f, rows, :] = upper_part(flux[f], cell, half, spread)
            flux = flux_along(cells, speed, pressure, 1)
            rim_cells = []
            for f in range(NF):
                at = 8 * level + f
                lower = ghost[8 * tile : 8 * tile + 8, at : at + 1]
                upper = ghost[16 + 8 * tile : 24 + 8 * tile, at : at + 1]
                rim_cells.append(jnp.where(half_row, upper, lower))
            rim_speed, rim_pressure = derived(rim_cells)
            rim_flux = flux_along(rim_cells, rim_speed, rim_pressure, 1)
            half_t, spread_t = 0.5 * inv, diffusion * inv * inv
            centre = 2.0 * diffusion * (1.0 + inv * inv) + 2.0 * spread
            for f in range(NF):
                full = jnp.concatenate([cells[f], rim_cells[f]], axis=1) if f else None
                whole = None
                if flux[f] is not None:
                    whole = jnp.concatenate([flux[f], rim_flux[f]], axis=1)
                give_up = lower_part(whole, full, half_t, spread_t)
                give_down = upper_part(whole, full, half_t, spread_t)
                width = rows_t + 128
                total = sums[f] + pltpu.roll(give_up, 1, axis=1)[:, :rows_t]
                total = total - pltpu.roll(give_down, width - 1, axis=1)[:, :rows_t]
                if f:
                    total = total - centre * cells[f]
                slope[level, f, rows, :] = total

    row = iota((rows_p, rows_t), 0)
    for level in range(2):
        start, now = (low0, low) if level == 0 else (high0, high)
        for f in range(NF):
            lower = pltpu.roll(down[level, f], 1, axis=0)
            lower = jnp.where(row == 0, rim_low[f][level : level + 1, :], lower)
            upper = pltpu.roll(up[level, f], rows_p - 1, axis=0)
            upper = jnp.where(row == rows_p - 1, rim_high[f][2 + level : 3 + level, :], upper)
            k = slope[level, f] + lower - upper
            if last:
                acc = acc_low if level == 0 else acc_high
                value = start[f] + (time_step / 6.0) * (acc[f] + k)
                if f == 0:
                    density_out[0, level] = value
                elif f < 4:
                    momentum_out[0, f - 1, level] = value
                else:
                    magnetic_out[0, f - 4, level] = value
                continue
            acc_out = acc_low_out if level == 0 else acc_high_out
            if stage == 1:
                acc_out[f] = k
            else:
                acc_out[f] = (acc_low if level == 0 else acc_high)[f] + 2.0 * k
            step = time_step if stage == 3 else 0.5 * time_step
            value = start[f] + step * k
            (low_out if level == 0 else high_out)[f] = value
            send_rows(first_out, last_out, level, f, value)
    if not last:
        new_low = low_out[...].reshape(NF * rows_p, rows_t)
        new_high = high_out[...].reshape(NF * rows_p, rows_t)
        answer_into(msg_out, new_low, new_high, corner[...], rowmask[...])


def body(
    density, momentum, magnetic, partner_device, partner_phi, partner_theta, partner_weight, border_turn
):
    _, rows_r, rows_p, rows_t = density.shape
    n_ang, n_rad = lax.axis_size("ang"), lax.axis_size("rad")
    f32 = jnp.float32
    vmem = pl.BlockSpec(memory_space=pltpu.VMEM)
    smem = pl.BlockSpec(memory_space=pltpu.SMEM)

    def shape(*dims):
        return jax.ShapeDtypeStruct(dims, f32)

    def call(kernel, ins, outs, scratch=(), name=None, scalars=0):
        return pl.pallas_call(
            kernel,
            out_shape=outs,
            in_specs=[smem] * scalars + [vmem] * (len(ins) - scalars),
            out_specs=[vmem] * len(outs),
            scratch_shapes=list(scratch),
            interpret=INTERPRET,
            name=name,
        )(*ins)

    level = shape(NF, rows_p, rows_t)
    edge = shape(NF, 2, rows_t)
    message = shape(32, 1, 128)

    def shifted(value, axis, by):
        size = lax.axis_size(axis)
        return lax.ppermute(value, axis, [(i, (i + by) % size) for i in range(size)])

    def crossed(value):
        swap = lax.ppermute(value, "panel", [(0, 1), (1, 0)])
        return lax.all_to_all(swap, "ang", split_axis=0, concat_axis=0, tiled=True)

    def halos(low, high, first, final):
        return (
            shifted(high, "rad", 1),
            shifted(low, "rad", -1),
            shifted(final, "ang", 1),
            shifted(first, "ang", -1),
        )

    flags = jnp.stack([lax.axis_index("rad"), lax.axis_index("ang")]).astype(jnp.int32)
    theta = math.pi / 4 + (np.arange(rows_t) + 0.5) * (math.pi / 2 / rows_t)
    sines = jnp.asarray((1.0 / np.sin(theta)).astype(np.float32)).reshape(1, rows_t)

    low0, high0, first, final, ask, table = call(
        open_kernel,
        [
            density, momentum, magnetic, partner_device, partner_phi, partner_theta, partner_weight,
            border_turn, jnp.cos(border_turn), jnp.sin(border_turn),
        ],
        [level, level, edge, edge, message, shape(32, 128)],
        name="open",
    )
    around = halos(low0, high0, first, final)
    corner, rowmask, answer = call(
        asked_kernel,
        [crossed(ask), low0, high0],
        [shape(rows_t, 128), shape(rows_p, 128), message],
        name="asked",
    )
    low, high, sums = low0, high0, []
    scratch = [pltpu.VMEM((2, NF, rows_p, rows_t), f32) for _ in range(3)]
    for stage in range(1, 5):
        ins = [flags, sines, low0, high0, *around, crossed(answer), table]
        if stage > 1:
            ins += [low, high, *sums]
        if stage < 4:
            ins += [corner, rowmask]
            outs = [level, level, level, level, edge, edge, message]
        else:
            outs = [
                shape(1, rows_r, rows_p, rows_t),
                shape(1, 3, rows_r, rows_p, rows_t),
                shape(1, 3, rows_r, rows_p, rows_t),
            ]

        def kernel(*refs, stage=stage):
            stage_kernel(stage, n_rad, n_ang, *refs)

        result = call(kernel, ins, outs, scratch, name=f"stage{stage}", scalars=1)
        if stage == 4:
            return tuple(result)
        low, high, acc_low, acc_high, first, final, answer = result
        sums = [acc_low, acc_high]
        around = halos(low, high, first, final)


def solution(mesh):
    in_specs = (
        P("panel", "rad", "ang", None),
        P("panel", None, "rad", "ang", None),
        P("panel", None, "rad", "ang", None),
        P("panel", "ang", None),
        P("panel", "ang"),
        P("panel", "ang"),
        P("panel", "ang", None),
        P("panel", "ang"),
    )
    out_specs = (
        P("panel", "rad", "ang", None),
        P("panel", None, "rad", "ang", None),
        P("panel", None, "rad", "ang", None),
    )
    return jax.shard_map(body, mesh=mesh, in_specs=in_specs, out_specs=out_specs, check_vma=False)
```

```python
import math

import jax
import jax.numpy as jnp
import numpy as np
from jax import lax
from jax.experimental import pallas as pl
from jax.experimental.pallas import tpu as pltpu
from jax.sharding import PartitionSpec as P

time_step = 0.15
diffusion = 0.1
r_inner = 0.35
NF = 7
MIRROR = (1.0, -1.0, -1.0, -1.0, 1.0, 1.0, 1.0)
INTERPRET = False
SLOT = 16
HIGHEST = lax.Precision.HIGHEST


def iota(shape, dim):
    return lax.broadcasted_iota(jnp.int32, shape, dim)


def derived(cells):
    inverse = 1.0 / cells[0]
    speed = [cells[1 + c] * inverse for c in range(3)]
    pressure = cells[0] + 0.5 * (
        cells[4] * cells[4] + cells[5] * cells[5] + cells[6] * cells[6]
    )
    return speed, pressure


def flux_along(cells, speed, pressure, d):
    moment, magnet = cells[1:4], cells[4:7]
    out = [moment[d]]
    for c in range(3):
        term = moment[c] * speed[d] - magnet[c] * magnet[d]
        out.append(term + pressure if c == d else term)
    for c in range(3):
        out.append(None if c == d else speed[d] * magnet[c] - magnet[d] * speed[c])
    return out


def upper_part(flux, cell, half, spread):
    if cell is None:
        return half * flux
    if flux is None:
        return -(spread * cell)
    return half * flux - spread * cell


def lower_part(flux, cell, half, spread):
    if cell is None:
        return half * flux
    if flux is None:
        return spread * cell
    return half * flux + spread * cell


def place(rad, n_rad, level, rows_r):
    value = None
    for at in range(n_rad):
        radius = r_inner + (at * rows_r + level + 0.5) * ((1.0 - r_inner) / (rows_r * n_rad))
        item = jnp.float32(1.0 / radius)
        value = item if value is None else jnp.where(rad == at, item, value)
    return value


def answer_into(msg_ref, low, high, corner, rowmask):
    rows_p = rowmask.shape[0]
    parts = []
    for level in (low, high):
        product = jnp.dot(level, corner, precision=HIGHEST, preferred_element_type=jnp.float32)
        picked = product.reshape(NF, rows_p, 128) * rowmask[None]
        parts.append(jnp.sum(picked, axis=1))
        parts.append(jnp.zeros((1, 128), jnp.float32))
    both = jnp.concatenate(parts, axis=0)
    both = both + pltpu.roll(both, 64, axis=1)
    turned = both.T
    lanes = jnp.concatenate([turned, jnp.zeros((128, 128 - SLOT), jnp.float32)], axis=1)
    lane = iota((32, 128), 1)
    message = jnp.where(lane < SLOT, lanes[0:32], pltpu.roll(lanes[32:64], SLOT, axis=1))
    msg_ref[...] = message.reshape(msg_ref.shape)


def send_rows(first_ref, last_ref, level, f, value):
    first_ref[f, level : level + 1, :] = value[0:1, :]
    last_ref[f, level : level + 1, :] = value[value.shape[0] - 1 :, :]


def open_kernel(
    density, momentum, magnetic, device, phi, theta, weight, turn,
    low_ref, high_ref, first_ref, last_ref, ask_ref, table_ref,
):
    for level, ref in ((0, low_ref), (1, high_ref)):
        for f in range(NF):
            if f == 0:
                value = density[0, level]
            elif f < 4:
                value = momentum[0, f - 1, level]
            else:
                value = magnetic[0, f - 4, level]
            ref[f] = value
            send_rows(first_ref, last_ref, level, f, value)
    rows = device.shape[2]
    one, two = iota((rows, rows), 0), iota((rows, rows), 1)
    eye = one == two
    dev_row = device[0]
    dev_col = jnp.sum(jnp.where(eye, jnp.broadcast_to(dev_row, (rows, rows)), 0), axis=1, keepdims=True)
    same = dev_col == dev_row
    rank_row = jnp.sum(jnp.where(same & (one < two), 1, 0), axis=0, keepdims=True)
    rank_col = jnp.sum(jnp.where(same & (two < one), 1, 0), axis=1, keepdims=True)

    def column(row):
        return jnp.sum(jnp.where(eye, jnp.broadcast_to(row, (rows, rows)), 0.0), axis=1, keepdims=True)

    phi_col = column(phi[...].astype(jnp.float32))
    theta_col = column(theta[...].astype(jnp.float32))
    weights = weight[0]
    lane = iota((rows, 128), 1)
    items = [phi_col, theta_col] + [column(weights[c : c + 1, :]) for c in range(4)]
    record = jnp.zeros((rows, 128), jnp.float32)
    for at, item in enumerate(items):
        record = jnp.where(lane == at, item, record)
    asked = jnp.zeros((rows, 128), jnp.float32)
    for slot in range(2):
        placing = jnp.where((one == dev_row) & (rank_row == slot), 1.0, 0.0)
        moved = record if slot == 0 else pltpu.roll(record, 8, axis=1)
        asked = asked + jnp.dot(placing, moved, precision=HIGHEST, preferred_element_type=jnp.float32)
    ask_ref[...] = asked.reshape(ask_ref.shape)
    picks = jnp.where(((lane & 31) == dev_col) & ((lane >> 5) == rank_col) & (lane < 64), 1.0, 0.0)
    cosine = column(jnp.cos(turn[...]))
    sine = column(jnp.sin(turn[...]))
    picks = jnp.where(lane == 64, cosine, picks)
    table_ref[...] = jnp.where(lane == 65, sine, picks)


def asked_kernel(asked_ref, low_ref, high_ref, corner_ref, mask_ref, msg_ref):
    asked = asked_ref[...].reshape(32, 128)
    lane, sub = iota((32, 128), 1), iota((32, 128), 0)

    def row_of(at):
        total = jnp.zeros((32, 128), jnp.float32)
        for part in range(4):
            slot = part & 1
            col = asked[:, slot * 8 + at[part >> 1] : slot * 8 + at[part >> 1] + 1]
            total = jnp.where(lane == sub + 32 * part, col, total)
        return jnp.sum(total, axis=0, keepdims=True)

    phi_row = row_of((0, 0)).astype(jnp.int32)
    theta_row = row_of((1, 1)).astype(jnp.int32)
    near = row_of((2, 4))
    far = row_of((3, 5))
    cell = iota((corner_ref.shape[0], 128), 0)
    corner = jnp.where(cell == theta_row, near, jnp.where(cell == theta_row + 1, far, 0.0))
    corner_ref[...] = corner
    rows_p = mask_ref.shape[0]
    wanted = phi_row + jnp.where(iota((1, 128), 1) < 64, 0, 1)
    mask = jnp.where(iota((rows_p, 128), 0) == wanted, 1.0, 0.0)
    mask_ref[...] = mask
    rows_t = low_ref.shape[2]
    low = low_ref[...].reshape(NF * rows_p, rows_t)
    high = high_ref[...].reshape(NF * rows_p, rows_t)
    answer_into(msg_ref, low, high, corner, mask)


def stage_kernel(stage, n_rad, n_ang, *refs):
    last = stage == 4
    (sines, low0, high0, below, above, before, after, reply, table) = refs[:9]
    refs = refs[9:]
    if stage == 1:
        low, high = low0, high0
    else:
        low, high, acc_low, acc_high = refs[:4]
        refs = refs[4:]
    if last:
        density_out, momentum_out, magnetic_out = refs[:3]
        refs = refs[3:]
    else:
        corner, rowmask = refs[:2]
        low_out, high_out, acc_low_out, acc_high_out, first_out, last_out, msg_out = refs[2:9]
        refs = refs[9:]
    slope, up, down = refs
    rad, ang = lax.axis_index("rad"), lax.axis_index("ang")
    rows_p, rows_t = low.shape[1:]
    invs = [place(rad, n_rad, level, 2) for level in range(2)]

    got = reply[...].reshape(32, 128)
    picks = table[...]
    ghost = jnp.dot(picks[:, 0:32], got, precision=HIGHEST, preferred_element_type=jnp.float32)
    second = jnp.dot(picks[:, 32:64], got, precision=HIGHEST, preferred_element_type=jnp.float32)
    ghost = ghost + pltpu.roll(second, 128 - SLOT, axis=1)
    cosine, sine = picks[:, 64:65], picks[:, 65:66]
    lane = iota((32, 128), 1) & 7
    is_t = (lane == 2) | (lane == 5)
    is_p = (lane == 3) | (lane == 6)
    turned_t = cosine * ghost + sine * pltpu.roll(ghost, 127, axis=1)
    turned_p = cosine * ghost - sine * pltpu.roll(ghost, 1, axis=1)
    ghost = jnp.where(is_t, turned_t, jnp.where(is_p, turned_p, ghost))

    sine_row = sines[...]
    rim = []
    for f in range(NF):
        own = [low[f, 0:1, :], high[f, 0:1, :], low[f, rows_p - 1 :, :], high[f, rows_p - 1 :, :]]
        own = [MIRROR[f] * item for item in own]
        start = jnp.where(ang == 0, jnp.concatenate(own[:2], axis=0), before[f])
        end = jnp.where(ang == n_ang - 1, jnp.concatenate(own[2:], axis=0), after[f])
        rim.append(jnp.concatenate([start, end, start, end], axis=0))
    rim_row = iota((8, rows_t), 0) & 1
    rim_inv = jnp.where(rim_row == 0, invs[0], invs[1]) * sine_row
    speed, pressure = derived(rim)
    flux = flux_along(rim, speed, pressure, 2)
    rim_half, rim_spread = 0.5 * rim_inv, diffusion * rim_inv * rim_inv
    rim_low = [lower_part(flux[f], rim[f] if f else None, rim_half, rim_spread) for f in range(NF)]
    rim_high = [upper_part(flux[f], rim[f] if f else None, rim_half, rim_spread) for f in range(NF)]

    half_row = iota((8, 128), 1) < 64
    for tile in range(rows_p // 8):
        rows = slice(8 * tile, 8 * tile + 8)
        for level in range(2):
            mine, other = (low, high) if level == 0 else (high, low)
            far, wall = (below, rad == 0) if level == 0 else (above, rad == n_rad - 1)
            cells = [mine[f, rows, :] for f in range(NF)]
            sums = []
            outer = [jnp.where(wall, MIRROR[f] * cells[f], far[f, rows, :]) for f in range(NF)]
            speed, pressure = derived(outer)
            flux = flux_along(outer, speed, pressure, 0)
            part = lower_part if level == 0 else upper_part
            for f in range(NF):
                sums.append(part(flux[f], outer[f] if f else None, 0.5, diffusion))
            inner = [other[f, rows, :] for f in range(NF)]
            speed, pressure = derived(inner)
            flux = flux_along(inner, speed, pressure, 0)
            part = upper_part if level == 0 else lower_part
            for f in range(NF):
                item = part(flux[f], inner[f] if f else None, 0.5, diffusion)
                sums[f] = sums[f] - item if level == 0 else item - sums[f]
            speed, pressure = derived(cells)
            inv = invs[level]
            inv_sine = inv * sine_row
            half, spread = 0.5 * inv_sine, diffusion * inv_sine * inv_sine
            flux = flux_along(cells, speed, pressure, 2)
            for f in range(NF):
                cell = cells[f] if f else None
                down[level, f, rows, :] = lower_part(flux[f], cell, half, spread)
                up[level, f, rows, :] = upper_part(flux[f], cell, half, spread)
            flux = flux_along(cells, speed, pressure, 1)
            rim_cells = []
            for f in range(NF):
                at = 8 * level + f
                lower = ghost[8 * tile : 8 * tile + 8, at : at + 1]
                upper = ghost[16 + 8 * tile : 24 + 8 * tile, at : at + 1]
                rim_cells.append(jnp.where(half_row, upper, lower))
            rim_speed, rim_pressure = derived(rim_cells)
            rim_flux = flux_along(rim_cells, rim_speed, rim_pressure, 1)
            half_t, spread_t = 0.5 * inv, diffusion * inv * inv
            centre = 2.0 * diffusion * (1.0 + inv * inv) + 2.0 * spread
            for f in range(NF):
                full = jnp.concatenate([cells[f], rim_cells[f]], axis=1) if f else None
                whole = None
                if flux[f] is not None:
                    whole = jnp.concatenate([flux[f], rim_flux[f]], axis=1)
                give_up = lower_part(whole, full, half_t, spread_t)
                give_down = upper_part(whole, full, half_t, spread_t)
                width = rows_t + 128
                total = sums[f] + pltpu.roll(give_up, 1, axis=1)[:, :rows_t]
                total = total - pltpu.roll(give_down, width - 1, axis=1)[:, :rows_t]
                if f:
                    total = total - centre * cells[f]
                slope[level, f, rows, :] = total

    row = iota((rows_p, rows_t), 0)
    for level in range(2):
        start, _ = (low0, low) if level == 0 else (high0, high)
        for f in range(NF):
            lower = pltpu.roll(down[level, f], 1, axis=0)
            lower = jnp.where(row == 0, rim_low[f][level : level + 1, :], lower)
            upper = pltpu.roll(up[level, f], rows_p - 1, axis=0)
            upper = jnp.where(row == rows_p - 1, rim_high[f][2 + level : 3 + level, :], upper)
            k = slope[level, f] + lower - upper
            if last:
                acc = acc_low if level == 0 else acc_high
                value = start[f] + (time_step / 6.0) * (acc[f] + k)
                if f == 0:
                    density_out[0, level] = value
                elif f < 4:
                    momentum_out[0, f - 1, level] = value
                else:
                    magnetic_out[0, f - 4, level] = value
                continue
            acc_out = acc_low_out if level == 0 else acc_high_out
            if stage == 1:
                acc_out[f] = k
            else:
                acc_out[f] = (acc_low if level == 0 else acc_high)[f] + 2.0 * k
            step = time_step if stage == 3 else 0.5 * time_step
            value = start[f] + step * k
            (low_out if level == 0 else high_out)[f] = value
            send_rows(first_out, last_out, level, f, value)
    if not last:
        new_low = low_out[...].reshape(NF * rows_p, rows_t)
        new_high = high_out[...].reshape(NF * rows_p, rows_t)
        answer_into(msg_out, new_low, new_high, corner[...], rowmask[...])


def body(
    density, momentum, magnetic, partner_device, partner_phi, partner_theta, partner_weight, border_turn
):
    _, rows_r, rows_p, rows_t = density.shape
    n_ang, n_rad = lax.axis_size("ang"), lax.axis_size("rad")
    f32 = jnp.float32
    vmem = pl.BlockSpec(memory_space=pltpu.VMEM)

    def shape(*dims, final=False):
        return jax.ShapeDtypeStruct(dims, f32) if final or INTERPRET else pltpu.VMEM(dims, f32)

    def held(value):
        return value if INTERPRET else pltpu.with_memory_space_constraint(value, pltpu.VMEM)

    def call(kernel, ins, outs, scratch=(), plain=0):
        return pl.pallas_call(
            kernel,
            out_shape=outs,
            in_specs=[vmem] * len(ins),
            out_specs=[vmem] * len(outs),
            scratch_shapes=list(scratch),
            interpret=INTERPRET,
            compiler_params=pltpu.CompilerParams(vmem_limit_bytes=None if plain > 1 else 12 << 20),
        )(*[item if at < plain else held(item) for at, item in enumerate(ins)])

    level = shape(NF, rows_p, rows_t)
    edge = shape(NF, 2, rows_t)
    message = shape(32, 1, 128)

    def shifted(value, axis, by):
        size = lax.axis_size(axis)
        return held(lax.ppermute(value, axis, [(i, (i + by) % size) for i in range(size)]))

    def crossed(value):
        swap = held(lax.ppermute(value, "panel", [(0, 1), (1, 0)]))
        return held(lax.all_to_all(swap, "ang", split_axis=0, concat_axis=0, tiled=True))

    def halos(low, high, first, final):
        items = ((high, "rad", 1), (low, "rad", -1), (final, "ang", 1), (first, "ang", -1))
        out = []
        for item in items:
            out.append(shifted(*item))
        return out

    theta = math.pi / 4 + (np.arange(rows_t) + 0.5) * (math.pi / 2 / rows_t)
    sines = jnp.asarray((1.0 / np.sin(theta)).astype(np.float32)).reshape(1, rows_t)

    low0, high0, first, final, ask, table = call(
        open_kernel,
        [
            density, momentum, magnetic, jnp.swapaxes(partner_device, 1, 2), partner_phi, partner_theta,
            jnp.swapaxes(partner_weight, 1, 2), border_turn,
        ],
        [level, level, edge, edge, message, shape(32, 128)],
        plain=8,
    )
    around = halos(low0, high0, first, final)
    corner, rowmask, answer = call(
        asked_kernel, [crossed(ask), low0, high0], [shape(rows_t, 128), shape(rows_p, 128), message]
    )
    low, high, sums = low0, high0, []
    scratch = [pltpu.VMEM((2, NF, rows_p, rows_t), f32) for _ in range(3)]
    for stage in range(1, 5):
        ins = [sines, low0, high0, *around, crossed(answer), table]
        if stage > 1:
            ins += [low, high, *sums]
        if stage < 4:
            ins += [corner, rowmask]
            outs = [level, level, level, level, edge, edge, message]
        else:
            outs = [
                shape(1, rows_r, rows_p, rows_t, final=True),
                shape(1, 3, rows_r, rows_p, rows_t, final=True),
                shape(1, 3, rows_r, rows_p, rows_t, final=True),
            ]

        def kernel(*refs, stage=stage):
            stage_kernel(stage, n_rad, n_ang, *refs)

        result = call(kernel, ins, outs, scratch, plain=1)
        if stage == 4:
            return tuple(result)
        low, high, acc_low, acc_high, first, final, answer = result
        sums = [acc_low, acc_high]
        around = halos(low, high, first, final)


def solution(mesh):
    in_specs = (
        P("panel", "rad", "ang", None),
        P("panel", None, "rad", "ang", None),
        P("panel", None, "rad", "ang", None),
        P("panel", "ang", None),
        P("panel", "ang"),
        P("panel", "ang"),
        P("panel", "ang", None),
        P("panel", "ang"),
    )
    out_specs = (
        P("panel", "rad", "ang", None),
        P("panel", None, "rad", "ang", None),
        P("panel", None, "rad", "ang", None),
    )
    return jax.shard_map(body, mesh=mesh, in_specs=in_specs, out_specs=out_specs, check_vma=False)
```

```python
import math

import jax
import jax.numpy as jnp
import numpy as np
from jax import lax
from jax.experimental import pallas as pl
from jax.experimental.pallas import tpu as pltpu
from jax.sharding import PartitionSpec as P

time_step = 0.15
diffusion = 0.1
r_inner = 0.35
NF = 7
MIRROR = (1.0, -1.0, -1.0, -1.0, 1.0, 1.0, 1.0)
INTERPRET = False
SLOT = 16
HIGHEST = lax.Precision.HIGHEST


def iota(shape, dim):
    return lax.broadcasted_iota(jnp.int32, shape, dim)


def derived(cells):
    inverse = 1.0 / cells[0]
    speed = [cells[1 + c] * inverse for c in range(3)]
    pressure = cells[0] + 0.5 * (
        cells[4] * cells[4] + cells[5] * cells[5] + cells[6] * cells[6]
    )
    return speed, pressure


def flux_along(cells, speed, pressure, d):
    moment, magnet = cells[1:4], cells[4:7]
    out = [moment[d]]
    for c in range(3):
        term = moment[c] * speed[d] - magnet[c] * magnet[d]
        out.append(term + pressure if c == d else term)
    for c in range(3):
        out.append(None if c == d else speed[d] * magnet[c] - magnet[d] * speed[c])
    return out


def upper_part(flux, cell, half, spread):
    if cell is None:
        return half * flux
    if flux is None:
        return -(spread * cell)
    return half * flux - spread * cell


def lower_part(flux, cell, half, spread):
    if cell is None:
        return half * flux
    if flux is None:
        return spread * cell
    return half * flux + spread * cell


def place(rad, n_rad, level, rows_r):
    value = None
    for at in range(n_rad):
        radius = r_inner + (at * rows_r + level + 0.5) * ((1.0 - r_inner) / (rows_r * n_rad))
        item = jnp.float32(1.0 / radius)
        value = item if value is None else jnp.where(rad == at, item, value)
    return value


def answer_into(msg_ref, low, high, corner, rowmask):
    rows_p = rowmask.shape[0]
    parts = []
    for level in (low, high):
        product = jnp.dot(level, corner, precision=HIGHEST, preferred_element_type=jnp.float32)
        picked = product.reshape(NF, rows_p, 128) * rowmask[None]
        parts.append(jnp.sum(picked, axis=1))
        parts.append(jnp.zeros((1, 128), jnp.float32))
    both = jnp.concatenate(parts, axis=0)
    both = both + pltpu.roll(both, 64, axis=1)
    turned = both.T
    lanes = jnp.concatenate([turned, jnp.zeros((128, 128 - SLOT), jnp.float32)], axis=1)
    lane = iota((32, 128), 1)
    message = jnp.where(lane < SLOT, lanes[0:32], pltpu.roll(lanes[32:64], SLOT, axis=1))
    msg_ref[...] = message.reshape(msg_ref.shape)


def send_rows(first_ref, last_ref, level, f, value):
    first_ref[f, level : level + 1, :] = value[0:1, :]
    last_ref[f, level : level + 1, :] = value[value.shape[0] - 1 :, :]


def open_kernel(
    density, momentum, magnetic, device, phi, theta, weight, turn, sines,
    low_ref, high_ref, first_ref, last_ref, ask_ref, table_ref, sines_ref,
):
    sines_ref[...] = sines[...]
    for level, ref in ((0, low_ref), (1, high_ref)):
        for f in range(NF):
            if f == 0:
                value = density[0, level]
            elif f < 4:
                value = momentum[0, f - 1, level]
            else:
                value = magnetic[0, f - 4, level]
            ref[f] = value
            send_rows(first_ref, last_ref, level, f, value)
    rows = device.shape[2]
    one, two = iota((rows, rows), 0), iota((rows, rows), 1)
    eye = one == two
    dev_row = device[0]
    dev_col = jnp.sum(jnp.where(eye, jnp.broadcast_to(dev_row, (rows, rows)), 0), axis=1, keepdims=True)
    same = dev_col == dev_row
    rank_row = jnp.sum(jnp.where(same & (one < two), 1, 0), axis=0, keepdims=True)
    rank_col = jnp.sum(jnp.where(same & (two < one), 1, 0), axis=1, keepdims=True)

    def column(row):
        return jnp.sum(jnp.where(eye, jnp.broadcast_to(row, (rows, rows)), 0.0), axis=1, keepdims=True)

    phi_col = column(phi[...].astype(jnp.float32))
    theta_col = column(theta[...].astype(jnp.float32))
    weights = weight[0]
    lane = iota((rows, 128), 1)
    items = [phi_col, theta_col] + [column(weights[c : c + 1, :]) for c in range(4)]
    record = jnp.zeros((rows, 128), jnp.float32)
    for at, item in enumerate(items):
        record = jnp.where(lane == at, item, record)
    asked = jnp.zeros((rows, 128), jnp.float32)
    for slot in range(2):
        placing = jnp.where((one == dev_row) & (rank_row == slot), 1.0, 0.0)
        moved = record if slot == 0 else pltpu.roll(record, 8, axis=1)
        asked = asked + jnp.dot(placing, moved, precision=HIGHEST, preferred_element_type=jnp.float32)
    ask_ref[...] = asked.reshape(ask_ref.shape)
    picks = jnp.where(((lane & 31) == dev_col) & ((lane >> 5) == rank_col) & (lane < 64), 1.0, 0.0)
    cosine = column(jnp.cos(turn[...]))
    sine = column(jnp.sin(turn[...]))
    picks = jnp.where(lane == 64, cosine, picks)
    table_ref[...] = jnp.where(lane == 65, sine, picks)


def asked_kernel(asked_ref, low_ref, high_ref, corner_ref, mask_ref, msg_ref):
    asked = asked_ref[...].reshape(32, 128)
    lane, sub = iota((32, 128), 1), iota((32, 128), 0)

    def row_of(at):
        total = jnp.zeros((32, 128), jnp.float32)
        for part in range(4):
            slot = part & 1
            col = asked[:, slot * 8 + at[part >> 1] : slot * 8 + at[part >> 1] + 1]
            total = jnp.where(lane == sub + 32 * part, col, total)
        return jnp.sum(total, axis=0, keepdims=True)

    phi_row = row_of((0, 0)).astype(jnp.int32)
    theta_row = row_of((1, 1)).astype(jnp.int32)
    near = row_of((2, 4))
    far = row_of((3, 5))
    cell = iota((corner_ref.shape[0], 128), 0)
    corner = jnp.where(cell == theta_row, near, jnp.where(cell == theta_row + 1, far, 0.0))
    corner_ref[...] = corner
    rows_p = mask_ref.shape[0]
    wanted = phi_row + jnp.where(iota((1, 128), 1) < 64, 0, 1)
    mask = jnp.where(iota((rows_p, 128), 0) == wanted, 1.0, 0.0)
    mask_ref[...] = mask
    rows_t = low_ref.shape[2]
    low = low_ref[...].reshape(NF * rows_p, rows_t)
    high = high_ref[...].reshape(NF * rows_p, rows_t)
    answer_into(msg_ref, low, high, corner, mask)


def ghost_kernel(reply, table, out_ref):
    got = reply[...].reshape(32, 128)
    picks = table[...]
    ghost = jnp.dot(picks[:, 0:32], got, precision=HIGHEST, preferred_element_type=jnp.float32)
    second = jnp.dot(picks[:, 32:64], got, precision=HIGHEST, preferred_element_type=jnp.float32)
    ghost = ghost + pltpu.roll(second, 128 - SLOT, axis=1)
    cosine, sine = picks[:, 64:65], picks[:, 65:66]
    lane = iota((32, 128), 1) & 7
    is_t = (lane == 2) | (lane == 5)
    is_p = (lane == 3) | (lane == 6)
    turned_t = cosine * ghost + sine * pltpu.roll(ghost, 127, axis=1)
    turned_p = cosine * ghost - sine * pltpu.roll(ghost, 1, axis=1)
    out_ref[...] = jnp.where(is_t, turned_t, jnp.where(is_p, turned_p, ghost))


def stage_kernel(stage, n_rad, n_ang, *refs):
    last = stage == 4
    (sines, low0, high0, below, above, before, after, ghosts) = refs[:8]
    refs = refs[8:]
    if stage == 1:
        low, high = low0, high0
    else:
        low, high, acc_low, acc_high = refs[:4]
        refs = refs[4:]
    if last:
        density_out, momentum_out, magnetic_out = refs[:3]
        refs = refs[3:]
    else:
        corner, rowmask = refs[:2]
        low_out, high_out, acc_low_out, acc_high_out, first_out, last_out, msg_out = refs[2:9]
        refs = refs[9:]
    slope, up, down = refs
    rad, ang = lax.axis_index("rad"), lax.axis_index("ang")
    rows_p, rows_t = low.shape[1:]
    invs = [place(rad, n_rad, level, 2) for level in range(2)]

    ghost = ghosts[...]

    sine_row = sines[...]
    rim = []
    for f in range(NF):
        own = [low[f, 0:1, :], high[f, 0:1, :], low[f, rows_p - 1 :, :], high[f, rows_p - 1 :, :]]
        own = [MIRROR[f] * item for item in own]
        start = jnp.where(ang == 0, jnp.concatenate(own[:2], axis=0), before[f])
        end = jnp.where(ang == n_ang - 1, jnp.concatenate(own[2:], axis=0), after[f])
        rim.append(jnp.concatenate([start, end, start, end], axis=0))
    rim_row = iota((8, rows_t), 0) & 1
    rim_inv = jnp.where(rim_row == 0, invs[0], invs[1]) * sine_row
    speed, pressure = derived(rim)
    flux = flux_along(rim, speed, pressure, 2)
    rim_half, rim_spread = 0.5 * rim_inv, diffusion * rim_inv * rim_inv
    rim_low = [lower_part(flux[f], rim[f] if f else None, rim_half, rim_spread) for f in range(NF)]
    rim_high = [upper_part(flux[f], rim[f] if f else None, rim_half, rim_spread) for f in range(NF)]

    half_row = iota((8, 128), 1) < 64
    for tile in range(rows_p // 8):
        rows = slice(8 * tile, 8 * tile + 8)
        for level in range(2):
            mine, other = (low, high) if level == 0 else (high, low)
            far, wall = (below, rad == 0) if level == 0 else (above, rad == n_rad - 1)
            cells = [mine[f, rows, :] for f in range(NF)]
            sums = []
            outer = [jnp.where(wall, MIRROR[f] * cells[f], far[f, rows, :]) for f in range(NF)]
            speed, pressure = derived(outer)
            flux = flux_along(outer, speed, pressure, 0)
            part = lower_part if level == 0 else upper_part
            for f in range(NF):
                sums.append(part(flux[f], outer[f] if f else None, 0.5, diffusion))
            inner = [other[f, rows, :] for f in range(NF)]
            speed, pressure = derived(inner)
            flux = flux_along(inner, speed, pressure, 0)
            part = upper_part if level == 0 else lower_part
            for f in range(NF):
                item = part(flux[f], inner[f] if f else None, 0.5, diffusion)
                sums[f] = sums[f] - item if level == 0 else item - sums[f]
            speed, pressure = derived(cells)
            inv = invs[level]
            inv_sine = inv * sine_row
            half, spread = 0.5 * inv_sine, diffusion * inv_sine * inv_sine
            flux = flux_along(cells, speed, pressure, 2)
            for f in range(NF):
                cell = cells[f] if f else None
                down[level, f, rows, :] = lower_part(flux[f], cell, half, spread)
                up[level, f, rows, :] = upper_part(flux[f], cell, half, spread)
            flux = flux_along(cells, speed, pressure, 1)
            rim_cells = []
            for f in range(NF):
                at = 8 * level + f
                lower = ghost[8 * tile : 8 * tile + 8, at : at + 1]
                upper = ghost[16 + 8 * tile : 24 + 8 * tile, at : at + 1]
                rim_cells.append(jnp.where(half_row, upper, lower))
            rim_speed, rim_pressure = derived(rim_cells)
            rim_flux = flux_along(rim_cells, rim_speed, rim_pressure, 1)
            half_t, spread_t = 0.5 * inv, diffusion * inv * inv
            centre = 2.0 * diffusion * (1.0 + inv * inv) + 2.0 * spread
            for f in range(NF):
                full = jnp.concatenate([cells[f], rim_cells[f]], axis=1) if f else None
                whole = None
                if flux[f] is not None:
                    whole = jnp.concatenate([flux[f], rim_flux[f]], axis=1)
                give_up = lower_part(whole, full, half_t, spread_t)
                give_down = upper_part(whole, full, half_t, spread_t)
                width = rows_t + 128
                total = sums[f] + pltpu.roll(give_up, 1, axis=1)[:, :rows_t]
                total = total - pltpu.roll(give_down, width - 1, axis=1)[:, :rows_t]
                if f:
                    total = total - centre * cells[f]
                slope[level, f, rows, :] = total

    row = iota((rows_p, rows_t), 0)
    for level in range(2):
        start, _ = (low0, low) if level == 0 else (high0, high)
        for f in range(NF):
            lower = pltpu.roll(down[level, f], 1, axis=0)
            lower = jnp.where(row == 0, rim_low[f][level : level + 1, :], lower)
            upper = pltpu.roll(up[level, f], rows_p - 1, axis=0)
            upper = jnp.where(row == rows_p - 1, rim_high[f][2 + level : 3 + level, :], upper)
            k = slope[level, f] + lower - upper
            if last:
                acc = acc_low if level == 0 else acc_high
                value = start[f] + (time_step / 6.0) * (acc[f] + k)
                if f == 0:
                    density_out[0, level] = value
                elif f < 4:
                    momentum_out[0, f - 1, level] = value
                else:
                    magnetic_out[0, f - 4, level] = value
                continue
            acc_out = acc_low_out if level == 0 else acc_high_out
            if stage == 1:
                acc_out[f] = k
            else:
                acc_out[f] = (acc_low if level == 0 else acc_high)[f] + 2.0 * k
            step = time_step if stage == 3 else 0.5 * time_step
            value = start[f] + step * k
            (low_out if level == 0 else high_out)[f] = value
            send_rows(first_out, last_out, level, f, value)
    if not last:
        new_low = low_out[...].reshape(NF * rows_p, rows_t)
        new_high = high_out[...].reshape(NF * rows_p, rows_t)
        answer_into(msg_out, new_low, new_high, corner[...], rowmask[...])


def body(
    density, momentum, magnetic, partner_device, partner_phi, partner_theta, partner_weight, border_turn
):
    _, rows_r, rows_p, rows_t = density.shape
    n_ang, n_rad = lax.axis_size("ang"), lax.axis_size("rad")
    f32 = jnp.float32
    vmem = pl.BlockSpec(memory_space=pltpu.VMEM)

    def shape(*dims, final=False):
        return jax.ShapeDtypeStruct(dims, f32) if final or INTERPRET else pltpu.VMEM(dims, f32)

    def held(value):
        return value if INTERPRET else pltpu.with_memory_space_constraint(value, pltpu.VMEM)

    def call(kernel, ins, outs, scratch=(), plain=0):
        return pl.pallas_call(
            kernel,
            out_shape=outs,
            in_specs=[vmem] * len(ins),
            out_specs=[vmem] * len(outs),
            scratch_shapes=list(scratch),
            interpret=INTERPRET,
            compiler_params=pltpu.CompilerParams(vmem_limit_bytes=None if plain > 1 else 12 << 20),
        )(*[item if at < plain else held(item) for at, item in enumerate(ins)])

    level = shape(NF, rows_p, rows_t)
    edge = shape(NF, 2, rows_t)
    message = shape(32, 1, 128)

    def shifted(value, axis, by):
        size = lax.axis_size(axis)
        return held(lax.ppermute(value, axis, [(i, (i + by) % size) for i in range(size)]))

    def crossed(value):
        swap = held(lax.ppermute(value, "panel", [(0, 1), (1, 0)]))
        return held(lax.all_to_all(swap, "ang", split_axis=0, concat_axis=0, tiled=True))

    def halos(low, high, first, final):
        items = ((high, "rad", 1), (low, "rad", -1), (final, "ang", 1), (first, "ang", -1))
        out = []
        for item in items:
            out.append(shifted(*item))
        return out

    theta = math.pi / 4 + (np.arange(rows_t) + 0.5) * (math.pi / 2 / rows_t)
    sines = jnp.asarray((1.0 / np.sin(theta)).astype(np.float32)).reshape(1, rows_t)

    low0, high0, first, final, ask, table, sines = call(
        open_kernel,
        [
            density, momentum, magnetic, jnp.swapaxes(partner_device, 1, 2), partner_phi, partner_theta,
            jnp.swapaxes(partner_weight, 1, 2), border_turn, sines,
        ],
        [level, level, edge, edge, message, shape(32, 128), shape(1, rows_t)],
        plain=9,
    )
    around = halos(low0, high0, first, final)
    corner, rowmask, answer = call(
        asked_kernel, [crossed(ask), low0, high0], [shape(rows_t, 128), shape(rows_p, 128), message]
    )
    low, high, sums = low0, high0, []
    scratch = [pltpu.VMEM((2, NF, rows_p, rows_t), f32) for _ in range(3)]
    for stage in range(1, 5):
        (ghosts,) = call(ghost_kernel, [crossed(answer), table], [shape(32, 128)])
        ins = [sines, low0, high0, *around, ghosts]
        if stage > 1:
            ins += [low, high, *sums]
        if stage < 4:
            ins += [corner, rowmask]
            outs = [level, level, level, level, edge, edge, message]
        else:
            outs = [
                shape(1, rows_r, rows_p, rows_t, final=True),
                shape(1, 3, rows_r, rows_p, rows_t, final=True),
                shape(1, 3, rows_r, rows_p, rows_t, final=True),
            ]

        def kernel(*refs, stage=stage):
            stage_kernel(stage, n_rad, n_ang, *refs)

        result = call(kernel, ins, outs, scratch)
        if stage == 4:
            return tuple(result)
        low, high, acc_low, acc_high, first, final, answer = result
        sums = [acc_low, acc_high]
        around = halos(low, high, first, final)


def solution(mesh):
    in_specs = (
        P("panel", "rad", "ang", None),
        P("panel", None, "rad", "ang", None),
        P("panel", None, "rad", "ang", None),
        P("panel", "ang", None),
        P("panel", "ang"),
        P("panel", "ang"),
        P("panel", "ang", None),
        P("panel", "ang"),
    )
    out_specs = (
        P("panel", "rad", "ang", None),
        P("panel", None, "rad", "ang", None),
        P("panel", None, "rad", "ang", None),
    )
    return jax.shard_map(body, mesh=mesh, in_specs=in_specs, out_specs=out_specs, check_vma=False)
```

```python
import math

import jax
import jax.numpy as jnp
import numpy as np
from jax import lax
from jax.experimental import pallas as pl
from jax.experimental.pallas import tpu as pltpu
from jax.sharding import PartitionSpec as P

time_step = 0.15
diffusion = 0.1
r_inner = 0.35
NF = 7
MIRROR = (1.0, -1.0, -1.0, -1.0, 1.0, 1.0, 1.0)
INTERPRET = False
EDGE = 4
SLOT = 16
HIGHEST = lax.Precision.HIGHEST


def iota(shape, dim):
    return lax.broadcasted_iota(jnp.int32, shape, dim)


def derived(cells):
    inverse = 1.0 / cells[0]
    speed = [cells[1 + c] * inverse for c in range(3)]
    pressure = cells[0] + 0.5 * (
        cells[4] * cells[4] + cells[5] * cells[5] + cells[6] * cells[6]
    )
    return speed, pressure


def flux_along(cells, speed, pressure, d):
    moment, magnet = cells[1:4], cells[4:7]
    out = [moment[d]]
    for c in range(3):
        term = moment[c] * speed[d] - magnet[c] * magnet[d]
        out.append(term + pressure if c == d else term)
    for c in range(3):
        out.append(None if c == d else speed[d] * magnet[c] - magnet[d] * speed[c])
    return out


def upper_part(flux, cell, half, spread):
    if cell is None:
        return half * flux
    if flux is None:
        return -(spread * cell)
    return half * flux - spread * cell


def lower_part(flux, cell, half, spread):
    if cell is None:
        return half * flux
    if flux is None:
        return spread * cell
    return half * flux + spread * cell


def place(rad, n_rad, level, rows_r):
    value = None
    for at in range(n_rad):
        radius = r_inner + (at * rows_r + level + 0.5) * ((1.0 - r_inner) / (rows_r * n_rad))
        item = jnp.float32(1.0 / radius)
        value = item if value is None else jnp.where(rad == at, item, value)
    return value


def answer_into(msg_ref, low, high, corner, rowmask):
    parts = []
    for level in (low, high):
        product = jnp.dot(level, corner, precision=HIGHEST, preferred_element_type=jnp.float32)
        product = product.reshape(NF, rowmask.shape[0], 128)
        picked = jnp.where(rowmask[None] > 0.5, product, 0.0)
        parts.append(jnp.sum(picked, axis=1))
        parts.append(jnp.zeros((1, 128), jnp.float32))
    both = jnp.concatenate(parts, axis=0)
    both = both + pltpu.roll(both, 64, axis=1)
    turned = both.T
    lanes = jnp.concatenate([turned, jnp.zeros((128, 128 - SLOT), jnp.float32)], axis=1)
    own = lanes[0:32] + pltpu.roll(lanes[32:64], SLOT, axis=1)
    before = pltpu.roll(pltpu.roll(own, 1, axis=0), 2 * SLOT, axis=1)
    after = pltpu.roll(pltpu.roll(own, 31, axis=0), 4 * SLOT, axis=1)
    msg_ref[...] = (own + before + after).reshape(msg_ref.shape)


def open_kernel(
    density, momentum, magnetic, device, phi, theta, weight, turn, sines,
    low_ref, high_ref, first_ref, last_ref, ask_ref, table_ref, sines_ref,
):
    sines_ref[...] = sines[...]
    for level, ref in ((0, low_ref), (1, high_ref)):
        for f in range(NF):
            if f == 0:
                value = density[0, level]
            elif f < 4:
                value = momentum[0, f - 1, level]
            else:
                value = magnetic[0, f - 4, level]
            ref[f] = value
            first_ref[f, EDGE * level : EDGE * level + EDGE, :] = value[:EDGE]
            last_ref[f, EDGE * level : EDGE * level + EDGE, :] = value[value.shape[0] - EDGE :]
    rows = device.shape[2]
    one, two = iota((rows, rows), 0), iota((rows, rows), 1)
    eye = one == two
    dev_row = device[0]
    dev_col = jnp.sum(jnp.where(eye, jnp.broadcast_to(dev_row, (rows, rows)), 0), axis=1, keepdims=True)
    same = dev_col == dev_row
    rank_row = jnp.sum(jnp.where(same & (one < two), 1, 0), axis=0, keepdims=True)
    rank_col = jnp.sum(jnp.where(same & (two < one), 1, 0), axis=1, keepdims=True)

    def column(row):
        return jnp.sum(jnp.where(eye, jnp.broadcast_to(row, (rows, rows)), 0.0), axis=1, keepdims=True)

    phi_col = column(phi[...].astype(jnp.float32))
    theta_col = column(theta[...].astype(jnp.float32))
    weights = weight[0]
    lane = iota((rows, 128), 1)
    items = [phi_col, theta_col] + [column(weights[c : c + 1, :]) for c in range(4)]
    record = jnp.zeros((rows, 128), jnp.float32)
    for at, item in enumerate(items):
        record = jnp.where(lane == at, item, record)
    asked = jnp.zeros((rows, 128), jnp.float32)
    for slot in range(2):
        placing = jnp.where((one == dev_row) & (rank_row == slot), 1.0, 0.0)
        moved = record if slot == 0 else pltpu.roll(record, 8, axis=1)
        asked = asked + jnp.dot(placing, moved, precision=HIGHEST, preferred_element_type=jnp.float32)
    ask_ref[...] = asked.reshape(ask_ref.shape)
    picks = jnp.where(((lane & 31) == dev_col) & ((lane >> 5) == rank_col) & (lane < 64), 1.0, 0.0)
    cosine = column(jnp.cos(turn[...]))
    sine = column(jnp.sin(turn[...]))
    picks = jnp.where(lane == 64, cosine, picks)
    picks = jnp.where(lane == 65, sine, picks)
    table_ref[...] = picks
    half = rows // 2
    for ref, at in ((first_ref, 0), (last_ref, half - EDGE)):
        ref[NF, 0:EDGE, 0:128] = picks[at : at + EDGE]
        ref[NF, EDGE : 2 * EDGE, 0:128] = picks[half + at : half + at + EDGE]
        ref[NF, :, 128:] = jnp.zeros((2 * EDGE, ref.shape[2] - 128), jnp.float32)


def asked_kernel(
    asked_ref, low_ref, high_ref, before_ref, after_ref, table_ref,
    corner_ref, mask_ref, low_out, high_out, table_out, msg_ref,
):
    own_rows = low_ref.shape[1]
    for level, ref, out in ((0, low_ref, low_out), (1, high_ref, high_out)):
        rows = slice(EDGE * level, EDGE * level + EDGE)
        for f in range(NF):
            out[f] = jnp.concatenate([before_ref[f, rows, :], ref[f], after_ref[f, rows, :]], axis=0)
    pieces = []
    for side in range(2):
        rows = slice(EDGE * side, EDGE * side + EDGE)
        half = own_rows * side
        pieces += [before_ref[NF, rows, 0:128], table_ref[half : half + own_rows, :], after_ref[NF, rows, 0:128]]
    table_out[...] = jnp.concatenate(pieces, axis=0)
    asked = asked_ref[...].reshape(32, 128)
    lane, sub = iota((32, 128), 1), iota((32, 128), 0)

    def row_of(at):
        total = jnp.zeros((32, 128), jnp.float32)
        for part in range(4):
            slot = part & 1
            col = asked[:, slot * 8 + at[part >> 1] : slot * 8 + at[part >> 1] + 1]
            total = jnp.where(lane == sub + 32 * part, col, total)
        return jnp.sum(total, axis=0, keepdims=True)

    phi_row = row_of((0, 0)).astype(jnp.int32)
    theta_row = row_of((1, 1)).astype(jnp.int32)
    near = row_of((2, 4))
    far = row_of((3, 5))
    cell = iota((corner_ref.shape[0], 128), 0)
    corner = jnp.where(cell == theta_row, near, jnp.where(cell == theta_row + 1, far, 0.0))
    corner_ref[...] = corner
    rows_p = mask_ref.shape[0]
    wanted = phi_row + EDGE + jnp.where(iota((1, 128), 1) < 64, 0, 1)
    mask = jnp.where(iota((rows_p, 128), 0) == wanted, 1.0, 0.0)
    mask_ref[...] = mask
    rows_t = low_ref.shape[2]
    low = low_out[...].reshape(NF * rows_p, rows_t)
    high = high_out[...].reshape(NF * rows_p, rows_t)
    answer_into(msg_ref, low, high, corner, mask)


def ghost_kernel(reply, table, out_ref):
    got = reply[...].reshape(32, 128)
    picks = table[...]
    rows = picks.shape[0]
    half = rows // 2
    ghost = jnp.dot(picks[:, 0:32], got, precision=HIGHEST, preferred_element_type=jnp.float32)
    second = jnp.dot(picks[:, 32:64], got, precision=HIGHEST, preferred_element_type=jnp.float32)
    ghost = ghost + pltpu.roll(second, 128 - SLOT, axis=1)
    row = iota((rows, 128), 0)
    row = jnp.where(row < half, row, row - half)
    before = pltpu.roll(ghost, 128 - 2 * SLOT, axis=1)
    after = pltpu.roll(ghost, 128 - 4 * SLOT, axis=1)
    ghost = jnp.where(row < EDGE, before, jnp.where(row < half - EDGE, ghost, after))
    cosine, sine = picks[:, 64:65], picks[:, 65:66]
    lane = iota((rows, 128), 1) & 7
    is_t = (lane == 2) | (lane == 5)
    is_p = (lane == 3) | (lane == 6)
    turned_t = cosine * ghost + sine * pltpu.roll(ghost, 127, axis=1)
    turned_p = cosine * ghost - sine * pltpu.roll(ghost, 1, axis=1)
    out_ref[...] = jnp.where(is_t, turned_t, jnp.where(is_p, turned_p, ghost))


def stage_kernel(stage, n_rad, n_ang, *refs):
    last = stage == 4
    (sines, low0, high0, below, above, ghosts) = refs[:6]
    refs = refs[6:]
    if stage == 1:
        low, high = low0, high0
    else:
        low, high, acc_low, acc_high = refs[:4]
        refs = refs[4:]
    if last:
        density_out, momentum_out, magnetic_out = refs[:3]
        refs = refs[3:]
    else:
        corner, rowmask = refs[:2]
        low_out, high_out, acc_low_out, acc_high_out, msg_out = refs[2:7]
        refs = refs[7:]
    slope, up, down = refs
    rad, ang = lax.axis_index("rad"), lax.axis_index("ang")
    rows_p, rows_t = low.shape[1:]
    invs = [place(rad, n_rad, level, 2) for level in range(2)]

    ghost = ghosts[...]

    sine_row = sines[...]
    first, final = EDGE, rows_p - EDGE - 1
    rim = []
    for f in range(NF):
        own = [level[f, at : at + 1, :] for at in (first, final) for level in (low, high)]
        rim.append(MIRROR[f] * jnp.concatenate(own + own, axis=0))
    rim_row = iota((8, rows_t), 0) & 1
    rim_inv = jnp.where(rim_row == 0, invs[0], invs[1]) * sine_row
    speed, pressure = derived(rim)
    flux = flux_along(rim, speed, pressure, 2)
    rim_half, rim_spread = 0.5 * rim_inv, diffusion * rim_inv * rim_inv
    rim_low = [lower_part(flux[f], rim[f] if f else None, rim_half, rim_spread) for f in range(NF)]
    rim_high = [upper_part(flux[f], rim[f] if f else None, rim_half, rim_spread) for f in range(NF)]

    half_row = iota((8, 128), 1) < 64
    for tile in range(rows_p // 8):
        rows = slice(8 * tile, 8 * tile + 8)
        for level in range(2):
            mine, other = (low, high) if level == 0 else (high, low)
            far, wall = (below, rad == 0) if level == 0 else (above, rad == n_rad - 1)
            cells = [mine[f, rows, :] for f in range(NF)]
            sums = []
            outer = [jnp.where(wall, MIRROR[f] * cells[f], far[f, rows, :]) for f in range(NF)]
            speed, pressure = derived(outer)
            flux = flux_along(outer, speed, pressure, 0)
            part = lower_part if level == 0 else upper_part
            for f in range(NF):
                sums.append(part(flux[f], outer[f] if f else None, 0.5, diffusion))
            inner = [other[f, rows, :] for f in range(NF)]
            speed, pressure = derived(inner)
            flux = flux_along(inner, speed, pressure, 0)
            part = upper_part if level == 0 else lower_part
            for f in range(NF):
                item = part(flux[f], inner[f] if f else None, 0.5, diffusion)
                sums[f] = sums[f] - item if level == 0 else item - sums[f]
            speed, pressure = derived(cells)
            inv = invs[level]
            inv_sine = inv * sine_row
            half, spread = 0.5 * inv_sine, diffusion * inv_sine * inv_sine
            flux = flux_along(cells, speed, pressure, 2)
            for f in range(NF):
                cell = cells[f] if f else None
                down[level, f, rows, :] = lower_part(flux[f], cell, half, spread)
                up[level, f, rows, :] = upper_part(flux[f], cell, half, spread)
            flux = flux_along(cells, speed, pressure, 1)
            rim_cells = []
            for f in range(NF):
                at = 8 * level + f
                lower = ghost[8 * tile : 8 * tile + 8, at : at + 1]
                upper = ghost[rows_p + 8 * tile : rows_p + 8 * tile + 8, at : at + 1]
                rim_cells.append(jnp.where(half_row, upper, lower))
            rim_speed, rim_pressure = derived(rim_cells)
            rim_flux = flux_along(rim_cells, rim_speed, rim_pressure, 1)
            half_t, spread_t = 0.5 * inv, diffusion * inv * inv
            centre = 2.0 * diffusion * (1.0 + inv * inv) + 2.0 * spread
            for f in range(NF):
                full = jnp.concatenate([cells[f], rim_cells[f]], axis=1) if f else None
                whole = None
                if flux[f] is not None:
                    whole = jnp.concatenate([flux[f], rim_flux[f]], axis=1)
                give_up = lower_part(whole, full, half_t, spread_t)
                give_down = upper_part(whole, full, half_t, spread_t)
                width = rows_t + 128
                total = sums[f] + pltpu.roll(give_up, 1, axis=1)[:, :rows_t]
                total = total - pltpu.roll(give_down, width - 1, axis=1)[:, :rows_t]
                if f:
                    total = total - centre * cells[f]
                slope[level, f, rows, :] = total

    row = iota((rows_p, rows_t), 0)
    wall_before = (row == first) & (ang == 0)
    wall_after = (row == final) & (ang == n_ang - 1)
    for level in range(2):
        start, _ = (low0, low) if level == 0 else (high0, high)
        for f in range(NF):
            lower = pltpu.roll(down[level, f], 1, axis=0)
            lower = jnp.where(wall_before, rim_low[f][level : level + 1, :], lower)
            upper = pltpu.roll(up[level, f], rows_p - 1, axis=0)
            upper = jnp.where(wall_after, rim_high[f][2 + level : 3 + level, :], upper)
            k = slope[level, f] + lower - upper
            if last:
                acc = acc_low if level == 0 else acc_high
                value = start[f] + (time_step / 6.0) * (acc[f] + k)
                value = pltpu.roll(value, rows_p - EDGE, axis=0)[: rows_p - 2 * EDGE]
                if f == 0:
                    density_out[0, level] = value
                elif f < 4:
                    momentum_out[0, f - 1, level] = value
                else:
                    magnetic_out[0, f - 4, level] = value
                continue
            acc_out = acc_low_out if level == 0 else acc_high_out
            if stage == 1:
                acc_out[f] = k
            else:
                acc_out[f] = (acc_low if level == 0 else acc_high)[f] + 2.0 * k
            step = time_step if stage == 3 else 0.5 * time_step
            value = start[f] + step * k
            (low_out if level == 0 else high_out)[f] = value
    if not last:
        new_low = low_out[...].reshape(NF * rows_p, rows_t)
        new_high = high_out[...].reshape(NF * rows_p, rows_t)
        answer_into(msg_out, new_low, new_high, corner[...], rowmask[...])


def body(
    density, momentum, magnetic, partner_device, partner_phi, partner_theta, partner_weight, border_turn
):
    _, rows_r, rows_p, rows_t = density.shape
    n_ang, n_rad = lax.axis_size("ang"), lax.axis_size("rad")
    f32 = jnp.float32
    vmem = pl.BlockSpec(memory_space=pltpu.VMEM)

    def shape(*dims, final=False):
        return jax.ShapeDtypeStruct(dims, f32) if final or INTERPRET else pltpu.VMEM(dims, f32)

    def held(value):
        return value if INTERPRET else pltpu.with_memory_space_constraint(value, pltpu.VMEM)

    def call(kernel, ins, outs, scratch=(), plain=0):
        return pl.pallas_call(
            kernel,
            out_shape=outs,
            in_specs=[vmem] * len(ins),
            out_specs=[vmem] * len(outs),
            scratch_shapes=list(scratch),
            interpret=INTERPRET,
            compiler_params=pltpu.CompilerParams(vmem_limit_bytes=None if plain > 1 else 12 << 20),
        )(*[item if at < plain else held(item) for at, item in enumerate(ins)])

    wide = rows_p + 2 * EDGE
    own_level = shape(NF, rows_p, rows_t)
    level = shape(NF, wide, rows_t)
    edge = shape(NF + 1, 2 * EDGE, rows_t)
    message = shape(32, 1, 128)

    def shifted(value, axis, by):
        size = lax.axis_size(axis)
        return held(lax.ppermute(value, axis, [(i, (i + by) % size) for i in range(size)]))

    def crossed(value):
        swap = held(lax.ppermute(value, "panel", [(0, 1), (1, 0)]))
        return held(lax.all_to_all(swap, "ang", split_axis=0, concat_axis=0, tiled=True))

    theta = math.pi / 4 + (np.arange(rows_t) + 0.5) * (math.pi / 2 / rows_t)
    sines = jnp.asarray((1.0 / np.sin(theta)).astype(np.float32)).reshape(1, rows_t)

    low0, high0, first, final, ask, table, sines = call(
        open_kernel,
        [
            density, momentum, magnetic, jnp.swapaxes(partner_device, 1, 2), partner_phi, partner_theta,
            jnp.swapaxes(partner_weight, 1, 2), border_turn, sines,
        ],
        [own_level, own_level, edge, edge, message, shape(32, 128), shape(1, rows_t)],
        plain=9,
    )
    before = shifted(final, "ang", 1)
    after = shifted(first, "ang", -1)
    corner, rowmask, low0, high0, table, answer = call(
        asked_kernel,
        [crossed(ask), low0, high0, before, after, table],
        [shape(rows_t, 128), shape(wide, 128), level, level, shape(2 * wide, 128), message],
    )
    low, high, sums = low0, high0, []
    scratch = [pltpu.VMEM((2, NF, wide, rows_t), f32) for _ in range(3)]
    for stage in range(1, 5):
        below = shifted(high, "rad", 1)
        above = shifted(low, "rad", -1)
        (ghosts,) = call(ghost_kernel, [crossed(answer), table], [shape(2 * wide, 128)])
        ins = [sines, low0, high0, below, above, ghosts]
        if stage > 1:
            ins += [low, high, *sums]
        if stage < 4:
            ins += [corner, rowmask]
            outs = [level, level, level, level, message]
        else:
            outs = [
                shape(1, rows_r, rows_p, rows_t, final=True),
                shape(1, 3, rows_r, rows_p, rows_t, final=True),
                shape(1, 3, rows_r, rows_p, rows_t, final=True),
            ]

        def kernel(*refs, stage=stage):
            stage_kernel(stage, n_rad, n_ang, *refs)

        result = call(kernel, ins, outs, scratch)
        if stage == 4:
            return tuple(result)
        low, high, acc_low, acc_high, answer = result
        sums = [acc_low, acc_high]


def solution(mesh):
    in_specs = (
        P("panel", "rad", "ang", None),
        P("panel", None, "rad", "ang", None),
        P("panel", None, "rad", "ang", None),
        P("panel", "ang", None),
        P("panel", "ang"),
        P("panel", "ang"),
        P("panel", "ang", None),
        P("panel", "ang"),
    )
    out_specs = (
        P("panel", "rad", "ang", None),
        P("panel", None, "rad", "ang", None),
        P("panel", None, "rad", "ang", None),
    )
    return jax.shard_map(body, mesh=mesh, in_specs=in_specs, out_specs=out_specs, check_vma=False)
```

```python
import math

import jax
import jax.numpy as jnp
import numpy as np
from jax import lax
from jax.experimental import pallas as pl
from jax.experimental.pallas import tpu as pltpu
from jax.sharding import PartitionSpec as P

time_step = 0.15
diffusion = 0.1
r_inner = 0.35
NF = 7
MIRROR = (1.0, -1.0, -1.0, -1.0, 1.0, 1.0, 1.0)
INTERPRET = False
EDGE = 4
SLOT = 16
HIGHEST = lax.Precision.HIGHEST


def iota(shape, dim):
    return lax.broadcasted_iota(jnp.int32, shape, dim)


def derived(cells):
    inverse = 1.0 / cells[0]
    speed = [cells[1 + c] * inverse for c in range(3)]
    pressure = cells[0] + 0.5 * (
        cells[4] * cells[4] + cells[5] * cells[5] + cells[6] * cells[6]
    )
    return speed, pressure


def stresses(cells, speed, pressure, pairs):
    moment, magnet = cells[1:4], cells[4:7]
    out = {}
    for c, d in pairs:
        term = moment[c] * speed[d] - magnet[c] * magnet[d]
        if c == d:
            out["T", c, d] = term + pressure
        else:
            out["T", c, d] = out["T", d, c] = term
            out["E", c, d] = speed[c] * magnet[d] - magnet[c] * speed[d]
    return out


def flux_along(cells, found, d):
    out = [(1, cells[1 + d])]
    for c in range(3):
        out.append((1, found["T", d, c]))
    for c in range(3):
        if c == d:
            out.append((0, None))
        elif c > d:
            out.append((1, found["E", d, c]))
        else:
            out.append((-1, found["E", c, d]))
    return out


ALL_PAIRS = ((0, 0), (0, 1), (0, 2), (1, 1), (1, 2), (2, 2))


def given(flux, cell, half, spread):
    sign, value = flux
    if cell is None:
        moved = half * value
        return moved, -moved
    spreading = spread * cell
    if not sign:
        return spreading, spreading
    moved = half * value
    plus, minus = spreading + moved, spreading - moved
    return (plus, minus) if sign > 0 else (minus, plus)


def inverse_radius(rad, n_rad, slot, rows_r):
    value = None
    for at in range(n_rad):
        level = 1 - (at & 1) if slot == 0 else at & 1
        radius = r_inner + (at * rows_r + level + 0.5) * ((1.0 - r_inner) / (rows_r * n_rad))
        item = jnp.float32(1.0 / radius)
        value = item if value is None else jnp.where(rad == at, item, value)
    return value


def partners(size, step):
    return [(i, (i ^ 1) if step == 0 else (((i + 1) ^ 1) - 1) % size) for i in range(size)]


def answer_into(msg_ref, low, high, corner, rowmask):
    cells = jnp.concatenate([low, high], axis=0)
    product = None
    for _ in range(3):
        part = cells.astype(jnp.bfloat16)
        cells = cells - part.astype(jnp.float32)
        item = jnp.dot(part, corner, preferred_element_type=jnp.float32)
        product = item if product is None else product + item
    product = product.reshape(2, NF, rowmask.shape[0], 128)
    picked = jnp.sum(jnp.where(rowmask != 0.0, product * rowmask, 0.0), axis=2)
    gap = jnp.zeros((1, 128), jnp.float32)
    parts = [picked[0], gap, picked[1], gap]
    both = jnp.concatenate(parts, axis=0)
    both = both + pltpu.roll(both, 64, axis=1)
    turned = both.T
    lanes = jnp.concatenate([turned, jnp.zeros((128, 128 - SLOT), jnp.float32)], axis=1)
    own = lanes[0:32] + pltpu.roll(lanes[32:64], SLOT, axis=1)
    before = pltpu.roll(pltpu.roll(own, 1, axis=0), 2 * SLOT, axis=1)
    after = pltpu.roll(pltpu.roll(own, 31, axis=0), 4 * SLOT, axis=1)
    msg_ref[...] = (own + before + after).reshape(msg_ref.shape)


def open_kernel(
    density, momentum, magnetic, device, phi, theta, weight, turn, sines,
    low_ref, high_ref, first_ref, last_ref, ask_ref, table_ref, sines_ref,
):
    sines_ref[...] = sines[...]
    odd = lax.axis_index("rad") & 1
    even_ang = (lax.axis_index("ang") & 1) == 0

    def edges(f, at, top, bottom):
        width = top.shape[1]
        first_ref[f, at : at + EDGE, 0:width] = jnp.where(even_ang, bottom, top)
        last_ref[f, at : at + EDGE, 0:width] = jnp.where(even_ang, top, bottom)

    for slot, ref in ((0, low_ref), (1, high_ref)):
        level = 1 - odd if slot == 0 else odd
        for f in range(NF):
            if f == 0:
                value = density[0, level]
            elif f < 4:
                value = momentum[0, f - 1, level]
            else:
                value = magnetic[0, f - 4, level]
            ref[f] = value
            edges(f, EDGE * slot, value[:EDGE], value[value.shape[0] - EDGE :])
    rows = device.shape[2]
    one, two = iota((rows, rows), 0), iota((rows, rows), 1)
    eye = one == two
    dev_row = device[0]
    dev_col = jnp.sum(jnp.where(eye, jnp.broadcast_to(dev_row, (rows, rows)), 0), axis=1, keepdims=True)
    same = dev_col == dev_row
    rank_row = jnp.sum(jnp.where(same & (one < two), 1, 0), axis=0, keepdims=True)
    rank_col = jnp.sum(jnp.where(same & (two < one), 1, 0), axis=1, keepdims=True)

    def column(row):
        return jnp.sum(jnp.where(eye, jnp.broadcast_to(row, (rows, rows)), 0.0), axis=1, keepdims=True)

    phi_col = column(phi[...].astype(jnp.float32))
    theta_col = column(theta[...].astype(jnp.float32))
    weights = weight[0]
    lane = iota((rows, 128), 1)
    items = [phi_col, theta_col] + [column(weights[c : c + 1, :]) for c in range(4)]
    record = jnp.zeros((rows, 128), jnp.float32)
    for at, item in enumerate(items):
        record = jnp.where(lane == at, item, record)
    asked = jnp.zeros((rows, 128), jnp.float32)
    for slot in range(2):
        placing = jnp.where((one == dev_row) & (rank_row == slot), 1.0, 0.0)
        moved = record if slot == 0 else pltpu.roll(record, 8, axis=1)
        asked = asked + jnp.dot(placing, moved, precision=HIGHEST, preferred_element_type=jnp.float32)
    ask_ref[...] = asked.reshape(ask_ref.shape)
    picks = jnp.where(((lane & 31) == dev_col) & ((lane >> 5) == rank_col) & (lane < 64), 1.0, 0.0)
    cosine = column(jnp.cos(turn[...]))
    sine = column(jnp.sin(turn[...]))
    picks = jnp.where(lane == 64, cosine, picks)
    picks = jnp.where(lane == 65, sine, picks)
    table_ref[...] = picks
    half = rows // 2
    for side in range(2):
        at = half * side
        edges(NF, EDGE * side, picks[at : at + EDGE], picks[at + half - EDGE : at + half])
    for ref in (first_ref, last_ref):
        ref[NF, :, 128:] = jnp.zeros((2 * EDGE, ref.shape[2] - 128), jnp.float32)


def asked_kernel(
    asked_ref, low_ref, high_ref, one_ref, two_ref, table_ref,
    corner_ref, mask_ref, low_out, high_out, table_out, msg_ref,
):
    own_rows = low_ref.shape[1]
    even_ang = (lax.axis_index("ang") & 1) == 0

    def beside(f, rows, width):
        one, two = one_ref[f, rows, 0:width], two_ref[f, rows, 0:width]
        return jnp.where(even_ang, two, one), jnp.where(even_ang, one, two)

    for level, ref, out in ((0, low_ref, low_out), (1, high_ref, high_out)):
        rows = slice(EDGE * level, EDGE * level + EDGE)
        for f in range(NF):
            before, after = beside(f, rows, ref.shape[2])
            out[f] = jnp.concatenate([before, ref[f], after], axis=0)
    pieces = []
    for side in range(2):
        rows = slice(EDGE * side, EDGE * side + EDGE)
        half = own_rows * side
        before, after = beside(NF, rows, 128)
        pieces += [before, table_ref[half : half + own_rows, :], after]
    table_out[...] = jnp.concatenate(pieces, axis=0)
    asked = asked_ref[...].reshape(32, 128)
    lane, sub = iota((32, 128), 1), iota((32, 128), 0)

    def row_of(at):
        total = jnp.zeros((32, 128), jnp.float32)
        for part in range(4):
            slot = part & 1
            col = asked[:, slot * 8 + at[part >> 1] : slot * 8 + at[part >> 1] + 1]
            total = jnp.where(lane == sub + 32 * part, col, total)
        return jnp.sum(total, axis=0, keepdims=True)

    phi_row = row_of((0, 0)).astype(jnp.int32) + EDGE
    theta_row = row_of((1, 1)).astype(jnp.int32) + jnp.where(iota((1, 128), 1) < 64, 0, 1)
    near = row_of((2, 3))
    far = row_of((4, 5))
    corner = jnp.where(iota((corner_ref.shape[0], 128), 0) == theta_row, 1.0, 0.0).astype(jnp.bfloat16)
    corner_ref[...] = corner
    rows_p = mask_ref.shape[0]
    at = iota((rows_p, 128), 0)
    mask = jnp.where(at == phi_row, near, jnp.where(at == phi_row + 1, far, 0.0))
    mask_ref[...] = mask
    rows_t = low_ref.shape[2]
    low = low_out[...].reshape(NF * rows_p, rows_t)
    high = high_out[...].reshape(NF * rows_p, rows_t)
    answer_into(msg_ref, low, high, corner, mask)


def ghost_kernel(reply, table, out_ref):
    got = reply[...].reshape(32, 128)
    picks = table[...]
    rows = picks.shape[0]
    half = rows // 2
    ghost = jnp.dot(picks[:, 0:32], got, precision=HIGHEST, preferred_element_type=jnp.float32)
    second = jnp.dot(picks[:, 32:64], got, precision=HIGHEST, preferred_element_type=jnp.float32)
    ghost = ghost + pltpu.roll(second, 128 - SLOT, axis=1)
    row = iota((rows, 128), 0)
    row = jnp.where(row < half, row, row - half)
    before = pltpu.roll(ghost, 128 - 2 * SLOT, axis=1)
    after = pltpu.roll(ghost, 128 - 4 * SLOT, axis=1)
    ghost = jnp.where(row < EDGE, before, jnp.where(row < half - EDGE, ghost, after))
    cosine, sine = picks[:, 64:65], picks[:, 65:66]
    lane = iota((rows, 128), 1) & 7
    is_t = (lane == 2) | (lane == 5)
    is_p = (lane == 3) | (lane == 6)
    turned_t = cosine * ghost + sine * pltpu.roll(ghost, 127, axis=1)
    turned_p = cosine * ghost - sine * pltpu.roll(ghost, 1, axis=1)
    out_ref[...] = jnp.where(is_t, turned_t, jnp.where(is_p, turned_p, ghost))


def stage_kernel(stage, n_rad, n_ang, *refs):
    last = stage == 4
    (sines, low0, high0, below, above, ghosts) = refs[:6]
    refs = refs[6:]
    if stage == 1:
        low, high = low0, high0
    else:
        low, high, acc_low, acc_high = refs[:4]
        refs = refs[4:]
    if last:
        density_out, momentum_out, magnetic_out = refs[:3]
        refs = refs[3:]
    else:
        corner, rowmask = refs[:2]
        low_out, high_out, acc_low_out, acc_high_out, msg_out = refs[2:7]
        refs = refs[7:]
    slope, up, down = refs
    rad, ang = lax.axis_index("rad"), lax.axis_index("ang")
    rows_p, rows_t = low.shape[1:]
    width = rows_t + 128
    invs = [inverse_radius(rad, n_rad, slot, 2) for slot in range(2)]
    outward = jnp.where((rad & 1) == 0, jnp.float32(0.5), jnp.float32(-0.5))
    wall = (rad == 0) | (rad == n_rad - 1)
    ghost = ghosts[...]
    sine_row = sines[...]
    first, final = EDGE, rows_p - EDGE - 1
    half_row = iota((8, 128), 1) < 64
    r_pairs = ((0, 0), (0, 1), (0, 2))
    t_pairs = ((0, 1), (1, 1), (1, 2))
    for tile in range(rows_p // 8):
        rows = slice(8 * tile, 8 * tile + 8)
        both = [[ref[f, rows, :] for f in range(NF)] for ref in (low, high)]
        found, r_flux = [], []
        for cells in both:
            found.append(stresses(cells, *derived(cells), ALL_PAIRS))
            r_flux.append(flux_along(cells, found[-1], 0))
        for slot in range(2):
            cells, inner, inner_flux = both[slot], both[1 - slot], r_flux[1 - slot]
            outer = [(below if slot == 0 else above)[f, rows, :] for f in range(NF)]
            if slot == 1:
                outer = [jnp.where(wall, MIRROR[f] * cells[f], outer[f]) for f in range(NF)]
            outer_flux = flux_along(outer, stresses(outer, *derived(outer), r_pairs), 0)
            half_r = outward if slot == 0 else -outward
            inv = invs[slot]
            inv_sine = inv * sine_row
            half, spread = 0.5 * inv_sine, diffusion * inv_sine * inv_sine
            half_t, spread_t = 0.5 * inv, diffusion * inv * inv
            centre = 2.0 * diffusion + 2.0 * spread_t + 2.0 * spread
            rim = []
            for f in range(NF):
                at = 8 * slot + f
                lower = ghost[8 * tile : 8 * tile + 8, at : at + 1]
                upper = ghost[rows_p + 8 * tile : rows_p + 8 * tile + 8, at : at + 1]
                rim.append(jnp.where(half_row, upper, lower))
            rim_flux = flux_along(rim, stresses(rim, *derived(rim), t_pairs), 1)
            t_flux = flux_along(cells, found[slot], 1)
            p_flux = flux_along(cells, found[slot], 2)
            for f in range(NF):
                cell = cells[f] if f else None
                down[slot, f, rows, :], up[slot, f, rows, :] = given(p_flux[f], cell, half, spread)
                total = None
                if r_flux[slot][f][0]:
                    total = half_r * (inner_flux[f][1] - outer_flux[f][1])
                if f:
                    item = diffusion * (inner[f] + outer[f]) - centre * cell
                    total = item if total is None else total + item
                whole = (t_flux[f][0], None)
                if t_flux[f][0]:
                    whole = (t_flux[f][0], jnp.concatenate([t_flux[f][1], rim_flux[f][1]], axis=1))
                full = jnp.concatenate([cell, rim[f]], axis=1) if f else None
                to_upper, to_lower = given(whole, full, half_t, spread_t)
                total = total + pltpu.roll(to_upper, 1, axis=1)[:, :rows_t]
                slope[slot, f, rows, :] = total + pltpu.roll(to_lower, width - 1, axis=1)[:, :rows_t]

    @pl.when(ang == 0)
    def _():
        for slot in range(2):
            for f in range(NF):
                down[slot, f, first - 1 : first, :] = MIRROR[f] * up[slot, f, first : first + 1, :]

    @pl.when(ang == n_ang - 1)
    def _():
        for slot in range(2):
            for f in range(NF):
                up[slot, f, final + 1 : final + 2, :] = MIRROR[f] * down[slot, f, final : final + 1, :]

    for slot in range(2):
        start = low0 if slot == 0 else high0
        for f in range(NF):
            k = slope[slot, f] + pltpu.roll(down[slot, f], 1, axis=0)
            k = k + pltpu.roll(up[slot, f], rows_p - 1, axis=0)
            if last:
                level = 1 - (rad & 1) if slot == 0 else rad & 1
                acc = acc_low if slot == 0 else acc_high
                value = start[f] + (time_step / 6.0) * (acc[f] + k)
                value = pltpu.roll(value, rows_p - EDGE, axis=0)[: rows_p - 2 * EDGE]
                if f == 0:
                    density_out[0, level] = value
                elif f < 4:
                    momentum_out[0, f - 1, level] = value
                else:
                    magnetic_out[0, f - 4, level] = value
                continue
            acc_out = acc_low_out if slot == 0 else acc_high_out
            if stage == 1:
                acc_out[f] = k
            else:
                acc_out[f] = (acc_low if slot == 0 else acc_high)[f] + 2.0 * k
            step = time_step if stage == 3 else 0.5 * time_step
            (low_out if slot == 0 else high_out)[f] = start[f] + step * k
    if not last:
        new_low = low_out[...].reshape(NF * rows_p, rows_t)
        new_high = high_out[...].reshape(NF * rows_p, rows_t)
        answer_into(msg_out, new_low, new_high, corner[...], rowmask[...])


def body(
    density, momentum, magnetic, partner_device, partner_phi, partner_theta, partner_weight, border_turn
):
    _, rows_r, rows_p, rows_t = density.shape
    n_ang, n_rad = lax.axis_size("ang"), lax.axis_size("rad")
    f32 = jnp.float32
    vmem = pl.BlockSpec(memory_space=pltpu.VMEM)

    def shape(*dims, final=False, dtype=f32):
        return jax.ShapeDtypeStruct(dims, dtype) if final or INTERPRET else pltpu.VMEM(dims, dtype)

    def held(value):
        return value if INTERPRET else pltpu.with_memory_space_constraint(value, pltpu.VMEM)

    def call(kernel, ins, outs, scratch=(), plain=0):
        return pl.pallas_call(
            kernel,
            out_shape=outs,
            in_specs=[vmem] * len(ins),
            out_specs=[vmem] * len(outs),
            scratch_shapes=list(scratch),
            interpret=INTERPRET,
            compiler_params=pltpu.CompilerParams(vmem_limit_bytes=None if plain > 1 else 12 << 20),
        )(*[item if at < plain else held(item) for at, item in enumerate(ins)])

    wide = rows_p + 2 * EDGE
    own_level = shape(NF, rows_p, rows_t)
    level = shape(NF, wide, rows_t)
    edge = shape(NF + 1, 2 * EDGE, rows_t)
    message = shape(32, 1, 128)

    def exchanged(value, axis, step):
        return held(lax.ppermute(value, axis, partners(lax.axis_size(axis), step)))

    def crossed(value):
        swap = held(lax.ppermute(value, "panel", [(0, 1), (1, 0)]))
        return held(lax.all_to_all(swap, "ang", split_axis=0, concat_axis=0, tiled=True))

    theta = math.pi / 4 + (np.arange(rows_t) + 0.5) * (math.pi / 2 / rows_t)
    sines = jnp.asarray((1.0 / np.sin(theta)).astype(np.float32)).reshape(1, rows_t)

    low0, high0, first, final, ask, table, sines = call(
        open_kernel,
        [
            density, momentum, magnetic, jnp.swapaxes(partner_device, 1, 2), partner_phi, partner_theta,
            jnp.swapaxes(partner_weight, 1, 2), border_turn, sines,
        ],
        [own_level, own_level, edge, edge, message, shape(32, 128), shape(1, rows_t)],
        plain=9,
    )
    one = exchanged(first, "ang", 0)
    two = exchanged(final, "ang", 1)
    corner, rowmask, low0, high0, table, answer = call(
        asked_kernel,
        [crossed(ask), low0, high0, one, two, table],
        [shape(rows_t, 128, dtype=jnp.bfloat16), shape(wide, 128), level, level, shape(2 * wide, 128), message],
    )
    low, high, sums = low0, high0, []
    scratch = [pltpu.VMEM((2, NF, wide, rows_t), f32) for _ in range(3)]
    for stage in range(1, 5):
        below = exchanged(low, "rad", 0)
        above = exchanged(high, "rad", 1)
        (ghosts,) = call(ghost_kernel, [crossed(answer), table], [shape(2 * wide, 128)])
        ins = [sines, low0, high0, below, above, ghosts]
        if stage > 1:
            ins += [low, high, *sums]
        if stage < 4:
            ins += [corner, rowmask]
            outs = [level, level, level, level, message]
        else:
            outs = [
                shape(1, rows_r, rows_p, rows_t, final=True),
                shape(1, 3, rows_r, rows_p, rows_t, final=True),
                shape(1, 3, rows_r, rows_p, rows_t, final=True),
            ]

        def kernel(*refs, stage=stage):
            stage_kernel(stage, n_rad, n_ang, *refs)

        result = call(kernel, ins, outs, scratch)
        if stage == 4:
            return tuple(result)
        low, high, acc_low, acc_high, answer = result
        sums = [acc_low, acc_high]


def solution(mesh):
    in_specs = (
        P("panel", "rad", "ang", None),
        P("panel", None, "rad", "ang", None),
        P("panel", None, "rad", "ang", None),
        P("panel", "ang", None),
        P("panel", "ang"),
        P("panel", "ang"),
        P("panel", "ang", None),
        P("panel", "ang"),
    )
    out_specs = (
        P("panel", "rad", "ang", None),
        P("panel", None, "rad", "ang", None),
        P("panel", None, "rad", "ang", None),
    )
    return jax.shard_map(body, mesh=mesh, in_specs=in_specs, out_specs=out_specs, check_vma=False)
```

```python
import math

import jax
import jax.numpy as jnp
import numpy as np
from jax import lax
from jax.experimental import pallas as pl
from jax.experimental.pallas import tpu as pltpu
from jax.sharding import PartitionSpec as P

time_step = 0.15
diffusion = 0.1
r_inner = 0.35
NF = 7
MIRROR = (1.0, -1.0, -1.0, -1.0, 1.0, 1.0, 1.0)
INTERPRET = False
EDGE = 4
SLOT = 16
HIGHEST = lax.Precision.HIGHEST


def iota(shape, dim):
    return lax.broadcasted_iota(jnp.int32, shape, dim)


def derived(cells):
    inverse = 1.0 / cells[0]
    speed = [cells[1 + c] * inverse for c in range(3)]
    pressure = cells[0] + 0.5 * (
        cells[4] * cells[4] + cells[5] * cells[5] + cells[6] * cells[6]
    )
    return speed, pressure


def stresses(cells, speed, pressure, pairs):
    moment, magnet = cells[1:4], cells[4:7]
    out = {}
    for c, d in pairs:
        term = moment[c] * speed[d] - magnet[c] * magnet[d]
        if c == d:
            out["T", c, d] = term + pressure
        else:
            out["T", c, d] = out["T", d, c] = term
            out["E", c, d] = speed[c] * magnet[d] - magnet[c] * speed[d]
    return out


def flux_along(cells, found, d):
    out = [(1, cells[1 + d])]
    for c in range(3):
        out.append((1, found["T", d, c]))
    for c in range(3):
        if c == d:
            out.append((0, None))
        elif c > d:
            out.append((1, found["E", d, c]))
        else:
            out.append((-1, found["E", c, d]))
    return out


ALL_PAIRS = ((0, 0), (0, 1), (0, 2), (1, 1), (1, 2), (2, 2))


def given(flux, cell, half, spread):
    sign, value = flux
    if cell is None:
        moved = half * value
        return moved, -moved
    spreading = spread * cell
    if not sign:
        return spreading, spreading
    moved = half * value
    plus, minus = spreading + moved, spreading - moved
    return (plus, minus) if sign > 0 else (minus, plus)


def inverse_radius(rad, n_rad, slot, rows_r):
    value = None
    for at in range(n_rad):
        level = 1 - (at & 1) if slot == 0 else at & 1
        radius = r_inner + (at * rows_r + level + 0.5) * ((1.0 - r_inner) / (rows_r * n_rad))
        item = jnp.float32(1.0 / radius)
        value = item if value is None else jnp.where(rad == at, item, value)
    return value


def partners(size, step):
    return [(i, (i ^ 1) if step == 0 else (((i + 1) ^ 1) - 1) % size) for i in range(size)]


def answer_part(cells, lanes, rowmask):
    at, tile = lanes & 127, lanes >> 7
    out = []
    for field in cells:
        total = None
        for row in range(0, rowmask.shape[0], 8):
            found = None
            for q in range(field.shape[1] // 128):
                item = jnp.take_along_axis(
                    field[row : row + 8, 128 * q : 128 * q + 128], at, axis=1, mode="promise_in_bounds"
                )
                found = item if found is None else jnp.where(tile == q, item, found)
            found = found * rowmask[row : row + 8, :]
            total = found if total is None else total + found
        out.append(jnp.sum(total, axis=0, keepdims=True))
    return out


def answer_into(msg_ref, picked):
    gap = jnp.zeros((1, 128), jnp.float32)
    parts = [*picked[0], gap, *picked[1], gap]
    both = jnp.concatenate(parts, axis=0)
    both = both + pltpu.roll(both, 64, axis=1)
    turned = both.T
    turned = jnp.concatenate([turned, jnp.zeros((128, 128 - SLOT), jnp.float32)], axis=1)
    own = turned[0:32] + pltpu.roll(turned[32:64], SLOT, axis=1)
    before = pltpu.roll(pltpu.roll(own, 1, axis=0), 2 * SLOT, axis=1)
    after = pltpu.roll(pltpu.roll(own, 31, axis=0), 4 * SLOT, axis=1)
    msg_ref[...] = (own + before + after).reshape(msg_ref.shape)


def open_kernel(
    density, momentum, magnetic, device, phi, theta, weight, turn, sines,
    low_ref, high_ref, first_ref, last_ref, ask_ref, table_ref, sines_ref,
):
    sines_ref[...] = sines[...]
    odd = lax.axis_index("rad") & 1
    even_ang = (lax.axis_index("ang") & 1) == 0

    def edges(f, at, top, bottom):
        width = top.shape[1]
        first_ref[f, at : at + EDGE, 0:width] = jnp.where(even_ang, bottom, top)
        last_ref[f, at : at + EDGE, 0:width] = jnp.where(even_ang, top, bottom)

    for slot, ref in ((0, low_ref), (1, high_ref)):
        level = 1 - odd if slot == 0 else odd
        for f in range(NF):
            if f == 0:
                value = density[0, level]
            elif f < 4:
                value = momentum[0, f - 1, level]
            else:
                value = magnetic[0, f - 4, level]
            ref[f] = value
            edges(f, EDGE * slot, value[:EDGE], value[value.shape[0] - EDGE :])
    rows = device.shape[2]
    one, two = iota((rows, rows), 0), iota((rows, rows), 1)
    eye = one == two
    dev_row = device[0]
    dev_col = jnp.sum(jnp.where(eye, jnp.broadcast_to(dev_row, (rows, rows)), 0), axis=1, keepdims=True)
    same = dev_col == dev_row
    rank_row = jnp.sum(jnp.where(same & (one < two), 1, 0), axis=0, keepdims=True)
    rank_col = jnp.sum(jnp.where(same & (two < one), 1, 0), axis=1, keepdims=True)

    def column(row):
        return jnp.sum(jnp.where(eye, jnp.broadcast_to(row, (rows, rows)), 0.0), axis=1, keepdims=True)

    phi_col = column(phi[...].astype(jnp.float32))
    theta_col = column(theta[...].astype(jnp.float32))
    weights = weight[0]
    lane = iota((rows, 128), 1)
    items = [phi_col, theta_col] + [column(weights[c : c + 1, :]) for c in range(4)]
    record = jnp.zeros((rows, 128), jnp.float32)
    for at, item in enumerate(items):
        record = jnp.where(lane == at, item, record)
    asked = jnp.zeros((rows, 128), jnp.float32)
    for slot in range(2):
        placing = jnp.where((one == dev_row) & (rank_row == slot), 1.0, 0.0)
        moved = record if slot == 0 else pltpu.roll(record, 8, axis=1)
        asked = asked + jnp.dot(placing, moved, precision=HIGHEST, preferred_element_type=jnp.float32)
    ask_ref[...] = asked.reshape(ask_ref.shape)
    picks = jnp.where(((lane & 31) == dev_col) & ((lane >> 5) == rank_col) & (lane < 64), 1.0, 0.0)
    cosine = column(jnp.cos(turn[...]))
    sine = column(jnp.sin(turn[...]))
    picks = jnp.where(lane == 64, cosine, picks)
    picks = jnp.where(lane == 65, sine, picks)
    table_ref[...] = picks
    half = rows // 2
    for side in range(2):
        at = half * side
        edges(NF, EDGE * side, picks[at : at + EDGE], picks[at + half - EDGE : at + half])
    for ref in (first_ref, last_ref):
        ref[NF, :, 128:] = jnp.zeros((2 * EDGE, ref.shape[2] - 128), jnp.float32)


def asked_kernel(
    asked_ref, low_ref, high_ref, one_ref, two_ref, table_ref,
    lanes_ref, mask_ref, low_out, high_out, table_out, msg_ref,
):
    own_rows = low_ref.shape[1]
    even_ang = (lax.axis_index("ang") & 1) == 0

    def beside(f, rows, width):
        one, two = one_ref[f, rows, 0:width], two_ref[f, rows, 0:width]
        return jnp.where(even_ang, two, one), jnp.where(even_ang, one, two)

    for level, ref, out in ((0, low_ref, low_out), (1, high_ref, high_out)):
        rows = slice(EDGE * level, EDGE * level + EDGE)
        for f in range(NF):
            before, after = beside(f, rows, ref.shape[2])
            out[f] = jnp.concatenate([ref[f], after, before], axis=0)
    pieces = []
    for side in range(2):
        rows = slice(EDGE * side, EDGE * side + EDGE)
        half = own_rows * side
        before, after = beside(NF, rows, 128)
        pieces += [table_ref[half : half + own_rows, :], after, before]
    table_out[...] = jnp.concatenate(pieces, axis=0)
    asked = asked_ref[...].reshape(32, 128)
    lane, sub = iota((32, 128), 1), iota((32, 128), 0)

    def row_of(at):
        total = jnp.zeros((32, 128), jnp.float32)
        for part in range(4):
            slot = part & 1
            col = asked[:, slot * 8 + at[part >> 1] : slot * 8 + at[part >> 1] + 1]
            total = jnp.where(lane == sub + 32 * part, col, total)
        return jnp.sum(total, axis=0, keepdims=True)

    phi_row = row_of((0, 0)).astype(jnp.int32)
    theta_row = row_of((1, 1)).astype(jnp.int32) + jnp.where(iota((1, 128), 1) < 64, 0, 1)
    near = row_of((2, 3))
    far = row_of((4, 5))
    lanes = jnp.broadcast_to(theta_row, (8, 128))
    lanes_ref[...] = lanes
    rows_p = mask_ref.shape[0]
    at = iota((rows_p, 128), 0)
    mask = jnp.where(at == phi_row, near, jnp.where(at == phi_row + 1, far, 0.0))
    mask_ref[...] = mask
    answer_into(
        msg_ref,
        [answer_part([ref[f] for f in range(NF)], lanes, mask) for ref in (low_ref, high_ref)],
    )


def ghost_kernel(reply, table, out_ref):
    got = reply[...].reshape(32, 128)
    picks = table[...]
    rows = picks.shape[0]
    half = rows // 2
    ghost = jnp.dot(picks[:, 0:32], got, precision=HIGHEST, preferred_element_type=jnp.float32)
    second = jnp.dot(picks[:, 32:64], got, precision=HIGHEST, preferred_element_type=jnp.float32)
    ghost = ghost + pltpu.roll(second, 128 - SLOT, axis=1)
    row = iota((rows, 128), 0)
    row = jnp.where(row < half, row, row - half)
    before = pltpu.roll(ghost, 128 - 2 * SLOT, axis=1)
    after = pltpu.roll(ghost, 128 - 4 * SLOT, axis=1)
    ghost = jnp.where(row < half - 2 * EDGE, ghost, jnp.where(row < half - EDGE, after, before))
    cosine, sine = picks[:, 64:65], picks[:, 65:66]
    lane = iota((rows, 128), 1) & 7
    is_t = (lane == 2) | (lane == 5)
    is_p = (lane == 3) | (lane == 6)
    turned_t = cosine * ghost + sine * pltpu.roll(ghost, 127, axis=1)
    turned_p = cosine * ghost - sine * pltpu.roll(ghost, 1, axis=1)
    out_ref[...] = jnp.where(is_t, turned_t, jnp.where(is_p, turned_p, ghost))


def stage_kernel(stage, n_rad, n_ang, *refs):
    last = stage == 4
    (sines, low0, high0, below, above, ghosts) = refs[:6]
    refs = refs[6:]
    if stage == 1:
        low, high = low0, high0
    else:
        low, high, acc_low, acc_high = refs[:4]
        refs = refs[4:]
    if last:
        density_out, momentum_out, magnetic_out = refs[:3]
        refs = refs[3:]
    else:
        lanes, rowmask = refs[:2]
        low_out, high_out, acc_low_out, acc_high_out, msg_out = refs[2:7]
        refs = refs[7:]
    slope, up, down = refs
    rad, ang = lax.axis_index("rad"), lax.axis_index("ang")
    rows_p, rows_t = low.shape[1:]
    width = rows_t + 128
    invs = [inverse_radius(rad, n_rad, slot, 2) for slot in range(2)]
    outward = jnp.where((rad & 1) == 0, jnp.float32(0.5), jnp.float32(-0.5))
    wall = (rad == 0) | (rad == n_rad - 1)
    ghost = ghosts[...]
    sine_row = sines[...]
    own = rows_p - 2 * EDGE
    half_row = iota((8, 128), 1) < 64
    r_pairs = ((0, 0), (0, 1), (0, 2))
    t_pairs = ((0, 1), (1, 1), (1, 2))
    p_pairs = ((0, 2), (1, 2), (2, 2))
    for tile in range(rows_p // 8):
        rows = slice(8 * tile, 8 * tile + 8)
        both = [[ref[f, rows, :] for f in range(NF)] for ref in (low, high)]
        if last and 8 * tile >= own:
            for slot in range(2):
                cells = both[slot]
                inv_sine = invs[slot] * sine_row
                half, spread = 0.5 * inv_sine, diffusion * inv_sine * inv_sine
                p_flux = flux_along(cells, stresses(cells, *derived(cells), p_pairs), 2)
                for f in range(NF):
                    cell = cells[f] if f else None
                    down[slot, f, rows, :], up[slot, f, rows, :] = given(p_flux[f], cell, half, spread)
            continue
        found, r_flux = [], []
        for cells in both:
            found.append(stresses(cells, *derived(cells), ALL_PAIRS))
            r_flux.append(flux_along(cells, found[-1], 0))
        for slot in range(2):
            cells, inner, inner_flux = both[slot], both[1 - slot], r_flux[1 - slot]
            outer = [(below if slot == 0 else above)[f, rows, :] for f in range(NF)]
            if slot == 1:
                outer = [jnp.where(wall, MIRROR[f] * cells[f], outer[f]) for f in range(NF)]
            outer_flux = flux_along(outer, stresses(outer, *derived(outer), r_pairs), 0)
            half_r = outward if slot == 0 else -outward
            inv = invs[slot]
            inv_sine = inv * sine_row
            half, spread = 0.5 * inv_sine, diffusion * inv_sine * inv_sine
            half_t, spread_t = 0.5 * inv, diffusion * inv * inv
            centre = 2.0 * diffusion + 2.0 * spread_t + 2.0 * spread
            rim = []
            for f in range(NF):
                at = 8 * slot + f
                lower = ghost[8 * tile : 8 * tile + 8, at : at + 1]
                upper = ghost[rows_p + 8 * tile : rows_p + 8 * tile + 8, at : at + 1]
                rim.append(jnp.where(half_row, upper, lower))
            rim_flux = flux_along(rim, stresses(rim, *derived(rim), t_pairs), 1)
            t_flux = flux_along(cells, found[slot], 1)
            p_flux = flux_along(cells, found[slot], 2)
            for f in range(NF):
                cell = cells[f] if f else None
                down[slot, f, rows, :], up[slot, f, rows, :] = given(p_flux[f], cell, half, spread)
                total = None
                if r_flux[slot][f][0]:
                    total = half_r * (inner_flux[f][1] - outer_flux[f][1])
                if f:
                    item = diffusion * (inner[f] + outer[f]) - centre * cell
                    total = item if total is None else total + item
                whole = (t_flux[f][0], None)
                if t_flux[f][0]:
                    whole = (t_flux[f][0], jnp.concatenate([t_flux[f][1], rim_flux[f][1]], axis=1))
                full = jnp.concatenate([cell, rim[f]], axis=1) if f else None
                to_upper, to_lower = given(whole, full, half_t, spread_t)
                total = total + pltpu.roll(to_upper, 1, axis=1)[:, :rows_t]
                slope[slot, f, rows, :] = total + pltpu.roll(to_lower, width - 1, axis=1)[:, :rows_t]

    @pl.when(ang == 0)
    def _():
        for slot in range(2):
            for f in range(NF):
                down[slot, f, rows_p - 1 :, :] = MIRROR[f] * up[slot, f, 0:1, :]

    @pl.when(ang == n_ang - 1)
    def _():
        for slot in range(2):
            for f in range(NF):
                up[slot, f, own : own + 1, :] = MIRROR[f] * down[slot, f, own - 1 : own, :]

    picked = []
    used = own if last else rows_p
    for slot in range(2):
        start = low0 if slot == 0 else high0
        values = []
        for f in range(NF):
            k = slope[slot, f, :used] + pltpu.roll(down[slot, f], 1, axis=0)[:used]
            k = k + pltpu.roll(up[slot, f], rows_p - 1, axis=0)[:used]
            if last:
                level = 1 - (rad & 1) if slot == 0 else rad & 1
                acc = acc_low if slot == 0 else acc_high
                value = start[f, :own] + (time_step / 6.0) * (acc[f] + k)
                if f == 0:
                    density_out[0, level] = value
                elif f < 4:
                    momentum_out[0, f - 1, level] = value
                else:
                    magnetic_out[0, f - 4, level] = value
                continue
            acc_out = acc_low_out if slot == 0 else acc_high_out
            if stage == 1:
                acc_out[f] = k[:own]
            else:
                acc_out[f] = (acc_low if slot == 0 else acc_high)[f] + 2.0 * k[:own]
            step = time_step if stage == 3 else 0.5 * time_step
            value = start[f] + step * k
            (low_out if slot == 0 else high_out)[f] = value
            values.append(value[:own])
        if not last:
            picked.append(answer_part(values, lanes[...], rowmask[...]))
    if not last:
        answer_into(msg_out, picked)


def body(
    density, momentum, magnetic, partner_device, partner_phi, partner_theta, partner_weight, border_turn
):
    _, rows_r, rows_p, rows_t = density.shape
    n_ang, n_rad = lax.axis_size("ang"), lax.axis_size("rad")
    f32 = jnp.float32
    vmem = pl.BlockSpec(memory_space=pltpu.VMEM)

    def shape(*dims, final=False, dtype=f32):
        return jax.ShapeDtypeStruct(dims, dtype) if final or INTERPRET else pltpu.VMEM(dims, dtype)

    def held(value):
        return value if INTERPRET else pltpu.with_memory_space_constraint(value, pltpu.VMEM)

    def call(kernel, ins, outs, scratch=(), plain=0):
        return pl.pallas_call(
            kernel,
            out_shape=outs,
            in_specs=[vmem] * len(ins),
            out_specs=[vmem] * len(outs),
            scratch_shapes=list(scratch),
            interpret=INTERPRET,
            compiler_params=pltpu.CompilerParams(vmem_limit_bytes=None if plain > 1 else 12 << 20),
        )(*[item if at < plain else held(item) for at, item in enumerate(ins)])

    wide = rows_p + 2 * EDGE
    own_level = shape(NF, rows_p, rows_t)
    level = shape(NF, wide, rows_t)
    edge = shape(NF + 1, 2 * EDGE, rows_t)
    message = shape(32, 1, 128)

    def exchanged(value, axis, step):
        return held(lax.ppermute(value, axis, partners(lax.axis_size(axis), step)))

    def crossed(value):
        swap = held(lax.ppermute(value, "panel", [(0, 1), (1, 0)]))
        return held(lax.all_to_all(swap, "ang", split_axis=0, concat_axis=0, tiled=True))

    theta = math.pi / 4 + (np.arange(rows_t) + 0.5) * (math.pi / 2 / rows_t)
    sines = jnp.asarray((1.0 / np.sin(theta)).astype(np.float32)).reshape(1, rows_t)

    low0, high0, first, final, ask, table, sines = call(
        open_kernel,
        [
            density, momentum, magnetic, jnp.swapaxes(partner_device, 1, 2), partner_phi, partner_theta,
            jnp.swapaxes(partner_weight, 1, 2), border_turn, sines,
        ],
        [own_level, own_level, edge, edge, message, shape(32, 128), shape(1, rows_t)],
        plain=9,
    )
    one = exchanged(first, "ang", 0)
    two = exchanged(final, "ang", 1)
    lanes, rowmask, low0, high0, table, answer = call(
        asked_kernel,
        [crossed(ask), low0, high0, one, two, table],
        [shape(8, 128, dtype=jnp.int32), shape(rows_p, 128), level, level, shape(2 * wide, 128), message],
    )
    low, high, sums = low0, high0, []
    scratch = [pltpu.VMEM((2, NF, wide, rows_t), f32) for _ in range(3)]
    for stage in range(1, 5):
        below = exchanged(low, "rad", 0)
        above = exchanged(high, "rad", 1)
        (ghosts,) = call(ghost_kernel, [crossed(answer), table], [shape(2 * wide, 128)])
        ins = [sines, low0, high0, below, above, ghosts]
        if stage > 1:
            ins += [low, high, *sums]
        if stage < 4:
            ins += [lanes, rowmask]
            outs = [level, level, own_level, own_level, message]
        else:
            outs = [
                shape(1, rows_r, rows_p, rows_t, final=True),
                shape(1, 3, rows_r, rows_p, rows_t, final=True),
                shape(1, 3, rows_r, rows_p, rows_t, final=True),
            ]

        def kernel(*refs, stage=stage):
            stage_kernel(stage, n_rad, n_ang, *refs)

        result = call(kernel, ins, outs, scratch)
        if stage == 4:
            return tuple(result)
        low, high, acc_low, acc_high, answer = result
        sums = [acc_low, acc_high]


def solution(mesh):
    in_specs = (
        P("panel", "rad", "ang", None),
        P("panel", None, "rad", "ang", None),
        P("panel", None, "rad", "ang", None),
        P("panel", "ang", None),
        P("panel", "ang"),
        P("panel", "ang"),
        P("panel", "ang", None),
        P("panel", "ang"),
    )
    out_specs = (
        P("panel", "rad", "ang", None),
        P("panel", None, "rad", "ang", None),
        P("panel", None, "rad", "ang", None),
    )
    return jax.shard_map(body, mesh=mesh, in_specs=in_specs, out_specs=out_specs, check_vma=False)
```

```python
import math

import jax
import jax.numpy as jnp
import numpy as np
from jax import lax
from jax.experimental import pallas as pl
from jax.experimental.pallas import tpu as pltpu
from jax.sharding import PartitionSpec as P

time_step = 0.15
diffusion = 0.1
r_inner = 0.35
NF = 7
MIRROR = (1.0, -1.0, -1.0, -1.0, 1.0, 1.0, 1.0)
INTERPRET = False
EDGE = 4
SLOT = 16
HIGHEST = lax.Precision.HIGHEST


def iota(shape, dim):
    return lax.broadcasted_iota(jnp.int32, shape, dim)


def derived(cells):
    inverse = 1.0 / cells[0]
    speed = [cells[1 + c] * inverse for c in range(3)]
    pressure = cells[0] + 0.5 * (
        cells[4] * cells[4] + cells[5] * cells[5] + cells[6] * cells[6]
    )
    return speed, pressure


def stresses(cells, speed, pressure, pairs):
    moment, magnet = cells[1:4], cells[4:7]
    out = {}
    for c, d in pairs:
        term = moment[c] * speed[d] - magnet[c] * magnet[d]
        if c == d:
            out["T", c, d] = term + pressure
        else:
            out["T", c, d] = out["T", d, c] = term
            out["E", c, d] = speed[c] * magnet[d] - magnet[c] * speed[d]
    return out


def flux_along(cells, found, d):
    out = [(1, cells[1 + d])]
    for c in range(3):
        out.append((1, found["T", d, c]))
    for c in range(3):
        if c == d:
            out.append((0, None))
        elif c > d:
            out.append((1, found["E", d, c]))
        else:
            out.append((-1, found["E", c, d]))
    return out


ALL_PAIRS = ((0, 0), (0, 1), (0, 2), (1, 1), (1, 2), (2, 2))


def given(flux, cell, half, spread):
    sign, value = flux
    if cell is None:
        moved = half * value
        return moved, -moved
    spreading = spread * cell
    if not sign:
        return spreading, spreading
    moved = half * value
    plus, minus = spreading + moved, spreading - moved
    return (plus, minus) if sign > 0 else (minus, plus)


def inverse_radius(rad, n_rad, slot, rows_r):
    value = None
    for at in range(n_rad):
        level = 1 - (at & 1) if slot == 0 else at & 1
        radius = r_inner + (at * rows_r + level + 0.5) * ((1.0 - r_inner) / (rows_r * n_rad))
        item = jnp.float32(1.0 / radius)
        value = item if value is None else jnp.where(rad == at, item, value)
    return value


def partners(size, step):
    return [(i, (i ^ 1) if step == 0 else (((i + 1) ^ 1) - 1) % size) for i in range(size)]


def answer_part(cells, lanes, rowmask):
    at, tile = lanes & 127, lanes >> 7
    out = []
    for field in cells:
        total = None
        for row in range(0, rowmask.shape[0], 8):
            found = None
            for q in range(field.shape[1] // 128):
                item = jnp.take_along_axis(
                    field[row : row + 8, 128 * q : 128 * q + 128], at, axis=1, mode="promise_in_bounds"
                )
                found = item if found is None else jnp.where(tile == q, item, found)
            found = found * rowmask[row : row + 8, :]
            total = found if total is None else total + found
        out.append(jnp.sum(total, axis=0, keepdims=True))
    return out


def answer_into(msg_ref, picked):
    gap = jnp.zeros((1, 128), jnp.float32)
    parts = [*picked[0], gap, *picked[1], gap]
    both = jnp.concatenate(parts, axis=0)
    both = both + pltpu.roll(both, 64, axis=1)
    turned = both.T
    turned = jnp.concatenate([turned, jnp.zeros((128, 128 - SLOT), jnp.float32)], axis=1)
    own = turned[0:32] + pltpu.roll(turned[32:64], SLOT, axis=1)
    before = pltpu.roll(pltpu.roll(own, 1, axis=0), 2 * SLOT, axis=1)
    after = pltpu.roll(pltpu.roll(own, 31, axis=0), 4 * SLOT, axis=1)
    msg_ref[...] = (own + before + after).reshape(msg_ref.shape)


def open_kernel(
    density, momentum, magnetic, device, phi, theta, weight, turn, sines,
    low_ref, high_ref, first_ref, last_ref, ask_ref, table_ref, sines_ref,
):
    sines_ref[...] = sines[...]
    odd = lax.axis_index("rad") & 1
    even_ang = (lax.axis_index("ang") & 1) == 0

    def edges(f, at, top, bottom):
        width = top.shape[1]
        first_ref[f, at : at + EDGE, 0:width] = jnp.where(even_ang, bottom, top)
        last_ref[f, at : at + EDGE, 0:width] = jnp.where(even_ang, top, bottom)

    for slot, ref in ((0, low_ref), (1, high_ref)):
        level = 1 - odd if slot == 0 else odd
        for f in range(NF):
            if f == 0:
                value = density[0, level]
            elif f < 4:
                value = momentum[0, f - 1, level]
            else:
                value = magnetic[0, f - 4, level]
            ref[f] = value
            edges(f, EDGE * slot, value[:EDGE], value[value.shape[0] - EDGE :])
    rows = device.shape[2]
    one, two = iota((rows, rows), 0), iota((rows, rows), 1)
    eye = one == two
    dev_row = device[0]
    dev_col = jnp.sum(jnp.where(eye, jnp.broadcast_to(dev_row, (rows, rows)), 0), axis=1, keepdims=True)
    same = dev_col == dev_row
    rank_row = jnp.sum(jnp.where(same & (one < two), 1, 0), axis=0, keepdims=True)
    rank_col = jnp.sum(jnp.where(same & (two < one), 1, 0), axis=1, keepdims=True)

    def column(row):
        return jnp.sum(jnp.where(eye, jnp.broadcast_to(row, (rows, rows)), 0.0), axis=1, keepdims=True)

    phi_col = column(phi[...].astype(jnp.float32))
    theta_col = column(theta[...].astype(jnp.float32))
    weights = weight[0]
    lane = iota((rows, 128), 1)
    items = [phi_col, theta_col] + [column(weights[c : c + 1, :]) for c in range(4)]
    record = jnp.zeros((rows, 128), jnp.float32)
    for at, item in enumerate(items):
        record = jnp.where(lane == at, item, record)
    asked = jnp.zeros((rows, 128), jnp.float32)
    for slot in range(2):
        placing = jnp.where((one == dev_row) & (rank_row == slot), 1.0, 0.0)
        moved = record if slot == 0 else pltpu.roll(record, 8, axis=1)
        asked = asked + jnp.dot(placing, moved, precision=HIGHEST, preferred_element_type=jnp.float32)
    ask_ref[...] = asked.reshape(ask_ref.shape)
    picks = jnp.where(((lane & 31) == dev_col) & ((lane >> 5) == rank_col) & (lane < 64), 1.0, 0.0)
    cosine = column(jnp.cos(turn[...]))
    sine = column(jnp.sin(turn[...]))
    picks = jnp.where(lane == 64, cosine, picks)
    picks = jnp.where(lane == 65, sine, picks)
    table_ref[...] = picks
    half = rows // 2
    for side in range(2):
        at = half * side
        edges(NF, EDGE * side, picks[at : at + EDGE], picks[at + half - EDGE : at + half])
    for ref in (first_ref, last_ref):
        ref[NF, :, 128:] = jnp.zeros((2 * EDGE, ref.shape[2] - 128), jnp.float32)


def asked_kernel(
    asked_ref, low_ref, high_ref, one_ref, two_ref, table_ref,
    lanes_ref, mask_ref, low_out, high_out, table_out, msg_ref,
):
    own_rows = low_ref.shape[1]
    even_ang = (lax.axis_index("ang") & 1) == 0

    def beside(f, rows, width):
        one, two = one_ref[f, rows, 0:width], two_ref[f, rows, 0:width]
        return jnp.where(even_ang, two, one), jnp.where(even_ang, one, two)

    for level, ref, out in ((0, low_ref, low_out), (1, high_ref, high_out)):
        rows = slice(EDGE * level, EDGE * level + EDGE)
        for f in range(NF):
            before, after = beside(f, rows, ref.shape[2])
            out[f] = jnp.concatenate([ref[f], after, before], axis=0)
    pieces = []
    for side in range(2):
        rows = slice(EDGE * side, EDGE * side + EDGE)
        half = own_rows * side
        before, after = beside(NF, rows, 128)
        pieces += [table_ref[half : half + own_rows, :], after, before]
    table_out[...] = jnp.concatenate(pieces, axis=0)
    asked = asked_ref[...].reshape(32, 128)
    lane, sub = iota((32, 128), 1), iota((32, 128), 0)

    def row_of(at):
        total = jnp.zeros((32, 128), jnp.float32)
        for part in range(4):
            slot = part & 1
            col = asked[:, slot * 8 + at[part >> 1] : slot * 8 + at[part >> 1] + 1]
            total = jnp.where(lane == sub + 32 * part, col, total)
        return jnp.sum(total, axis=0, keepdims=True)

    phi_row = row_of((0, 0)).astype(jnp.int32)
    theta_row = row_of((1, 1)).astype(jnp.int32) + jnp.where(iota((1, 128), 1) < 64, 0, 1)
    near = row_of((2, 3))
    far = row_of((4, 5))
    lanes = jnp.broadcast_to(theta_row, (8, 128))
    lanes_ref[...] = lanes
    rows_p = mask_ref.shape[0]
    at = iota((rows_p, 128), 0)
    mask = jnp.where(at == phi_row, near, jnp.where(at == phi_row + 1, far, 0.0))
    mask_ref[...] = mask
    answer_into(
        msg_ref,
        [answer_part([ref[f] for f in range(NF)], lanes, mask) for ref in (low_ref, high_ref)],
    )


def ghosts_of(reply, table):
    got = reply[...].reshape(32, 128)
    picks = table[...]
    rows = picks.shape[0]
    half = rows // 2
    ghost = jnp.dot(picks[:, 0:32], got, precision=HIGHEST, preferred_element_type=jnp.float32)
    second = jnp.dot(picks[:, 32:64], got, precision=HIGHEST, preferred_element_type=jnp.float32)
    ghost = ghost + pltpu.roll(second, 128 - SLOT, axis=1)
    row = iota((rows, 128), 0)
    row = jnp.where(row < half, row, row - half)
    before = pltpu.roll(ghost, 128 - 2 * SLOT, axis=1)
    after = pltpu.roll(ghost, 128 - 4 * SLOT, axis=1)
    ghost = jnp.where(row < half - 2 * EDGE, ghost, jnp.where(row < half - EDGE, after, before))
    cosine, sine = picks[:, 64:65], picks[:, 65:66]
    lane = iota((rows, 128), 1) & 7
    is_t = (lane == 2) | (lane == 5)
    is_p = (lane == 3) | (lane == 6)
    turned_t = cosine * ghost + sine * pltpu.roll(ghost, 127, axis=1)
    turned_p = cosine * ghost - sine * pltpu.roll(ghost, 1, axis=1)
    return jnp.where(is_t, turned_t, jnp.where(is_p, turned_p, ghost))


def stage_kernel(stage, n_rad, n_ang, *refs):
    last = stage == 4
    (sines, low0, high0, below, above, reply, table) = refs[:7]
    refs = refs[7:]
    if stage == 1:
        low, high = low0, high0
    else:
        low, high, acc_low, acc_high = refs[:4]
        refs = refs[4:]
    if last:
        density_out, momentum_out, magnetic_out = refs[:3]
        refs = refs[3:]
    else:
        lanes, rowmask = refs[:2]
        low_out, high_out, acc_low_out, acc_high_out, msg_out = refs[2:7]
        refs = refs[7:]
    slope, up, down = refs
    rad, ang = lax.axis_index("rad"), lax.axis_index("ang")
    rows_p, rows_t = low.shape[1:]
    width = rows_t + 128
    invs = [inverse_radius(rad, n_rad, slot, 2) for slot in range(2)]
    outward = jnp.where((rad & 1) == 0, jnp.float32(0.5), jnp.float32(-0.5))
    wall = (rad == 0) | (rad == n_rad - 1)
    ghost = ghosts_of(reply, table)
    sine_row = sines[...]
    own = rows_p - 2 * EDGE
    half_row = iota((8, 128), 1) < 64
    r_pairs = ((0, 0), (0, 1), (0, 2))
    t_pairs = ((0, 1), (1, 1), (1, 2))
    p_pairs = ((0, 2), (1, 2), (2, 2))
    for tile in range(rows_p // 8):
        rows = slice(8 * tile, 8 * tile + 8)
        both = [[ref[f, rows, :] for f in range(NF)] for ref in (low, high)]
        if last and 8 * tile >= own:
            for slot in range(2):
                cells = both[slot]
                inv_sine = invs[slot] * sine_row
                half, spread = 0.5 * inv_sine, diffusion * inv_sine * inv_sine
                p_flux = flux_along(cells, stresses(cells, *derived(cells), p_pairs), 2)
                for f in range(NF):
                    cell = cells[f] if f else None
                    down[slot, f, rows, :], up[slot, f, rows, :] = given(p_flux[f], cell, half, spread)
            continue
        found, r_flux = [], []
        for cells in both:
            found.append(stresses(cells, *derived(cells), ALL_PAIRS))
            r_flux.append(flux_along(cells, found[-1], 0))
        for slot in range(2):
            cells, inner, inner_flux = both[slot], both[1 - slot], r_flux[1 - slot]
            outer = [(below if slot == 0 else above)[f, rows, :] for f in range(NF)]
            if slot == 1:
                outer = [jnp.where(wall, MIRROR[f] * cells[f], outer[f]) for f in range(NF)]
            outer_flux = flux_along(outer, stresses(outer, *derived(outer), r_pairs), 0)
            half_r = outward if slot == 0 else -outward
            inv = invs[slot]
            inv_sine = inv * sine_row
            half, spread = 0.5 * inv_sine, diffusion * inv_sine * inv_sine
            half_t, spread_t = 0.5 * inv, diffusion * inv * inv
            centre = 2.0 * diffusion + 2.0 * spread_t + 2.0 * spread
            rim = []
            for f in range(NF):
                at = 8 * slot + f
                lower = ghost[8 * tile : 8 * tile + 8, at : at + 1]
                upper = ghost[rows_p + 8 * tile : rows_p + 8 * tile + 8, at : at + 1]
                rim.append(jnp.where(half_row, upper, lower))
            rim_flux = flux_along(rim, stresses(rim, *derived(rim), t_pairs), 1)
            t_flux = flux_along(cells, found[slot], 1)
            p_flux = flux_along(cells, found[slot], 2)
            for f in range(NF):
                cell = cells[f] if f else None
                down[slot, f, rows, :], up[slot, f, rows, :] = given(p_flux[f], cell, half, spread)
                total = None
                if r_flux[slot][f][0]:
                    total = half_r * (inner_flux[f][1] - outer_flux[f][1])
                if f:
                    item = diffusion * (inner[f] + outer[f]) - centre * cell
                    total = item if total is None else total + item
                whole = (t_flux[f][0], None)
                if t_flux[f][0]:
                    whole = (t_flux[f][0], jnp.concatenate([t_flux[f][1], rim_flux[f][1]], axis=1))
                full = jnp.concatenate([cell, rim[f]], axis=1) if f else None
                to_upper, to_lower = given(whole, full, half_t, spread_t)
                total = total + pltpu.roll(to_upper, 1, axis=1)[:, :rows_t]
                slope[slot, f, rows, :] = total + pltpu.roll(to_lower, width - 1, axis=1)[:, :rows_t]

    @pl.when(ang == 0)
    def _():
        for slot in range(2):
            for f in range(NF):
                down[slot, f, rows_p - 1 :, :] = MIRROR[f] * up[slot, f, 0:1, :]

    @pl.when(ang == n_ang - 1)
    def _():
        for slot in range(2):
            for f in range(NF):
                up[slot, f, own : own + 1, :] = MIRROR[f] * down[slot, f, own - 1 : own, :]

    picked = []
    used = own if last else rows_p
    for slot in range(2):
        start = low0 if slot == 0 else high0
        values = []
        for f in range(NF):
            k = slope[slot, f, :used] + pltpu.roll(down[slot, f], 1, axis=0)[:used]
            k = k + pltpu.roll(up[slot, f], rows_p - 1, axis=0)[:used]
            if last:
                level = 1 - (rad & 1) if slot == 0 else rad & 1
                acc = acc_low if slot == 0 else acc_high
                value = start[f, :own] + (time_step / 6.0) * (acc[f] + k)
                if f == 0:
                    density_out[0, level] = value
                elif f < 4:
                    momentum_out[0, f - 1, level] = value
                else:
                    magnetic_out[0, f - 4, level] = value
                continue
            acc_out = acc_low_out if slot == 0 else acc_high_out
            if stage == 1:
                acc_out[f] = k[:own]
            else:
                acc_out[f] = (acc_low if slot == 0 else acc_high)[f] + 2.0 * k[:own]
            step = time_step if stage == 3 else 0.5 * time_step
            value = start[f] + step * k
            (low_out if slot == 0 else high_out)[f] = value
            values.append(value[:own])
        if not last:
            picked.append(answer_part(values, lanes[...], rowmask[...]))
    if not last:
        answer_into(msg_out, picked)


def body(
    density, momentum, magnetic, partner_device, partner_phi, partner_theta, partner_weight, border_turn
):
    _, rows_r, rows_p, rows_t = density.shape
    n_ang, n_rad = lax.axis_size("ang"), lax.axis_size("rad")
    f32 = jnp.float32
    vmem = pl.BlockSpec(memory_space=pltpu.VMEM)

    def shape(*dims, final=False, dtype=f32):
        return jax.ShapeDtypeStruct(dims, dtype) if final or INTERPRET else pltpu.VMEM(dims, dtype)

    def held(value):
        return value if INTERPRET else pltpu.with_memory_space_constraint(value, pltpu.VMEM)

    def call(kernel, ins, outs, scratch=(), plain=0):
        return pl.pallas_call(
            kernel,
            out_shape=outs,
            in_specs=[vmem] * len(ins),
            out_specs=[vmem] * len(outs),
            scratch_shapes=list(scratch),
            interpret=INTERPRET,
            compiler_params=pltpu.CompilerParams(vmem_limit_bytes=None if plain > 1 else 12 << 20),
        )(*[item if at < plain else held(item) for at, item in enumerate(ins)])

    wide = rows_p + 2 * EDGE
    own_level = shape(NF, rows_p, rows_t)
    level = shape(NF, wide, rows_t)
    edge = shape(NF + 1, 2 * EDGE, rows_t)
    message = shape(32, 1, 128)

    def exchanged(value, axis, step):
        return held(lax.ppermute(value, axis, partners(lax.axis_size(axis), step)))

    def crossed(value):
        swap = held(lax.ppermute(value, "panel", [(0, 1), (1, 0)]))
        return held(lax.all_to_all(swap, "ang", split_axis=0, concat_axis=0, tiled=True))

    theta = math.pi / 4 + (np.arange(rows_t) + 0.5) * (math.pi / 2 / rows_t)
    sines = jnp.asarray((1.0 / np.sin(theta)).astype(np.float32)).reshape(1, rows_t)

    low0, high0, first, final, ask, table, sines = call(
        open_kernel,
        [
            density, momentum, magnetic, jnp.swapaxes(partner_device, 1, 2), partner_phi, partner_theta,
            jnp.swapaxes(partner_weight, 1, 2), border_turn, sines,
        ],
        [own_level, own_level, edge, edge, message, shape(32, 128), shape(1, rows_t)],
        plain=9,
    )
    one = exchanged(first, "ang", 0)
    two = exchanged(final, "ang", 1)
    lanes, rowmask, low0, high0, table, answer = call(
        asked_kernel,
        [crossed(ask), low0, high0, one, two, table],
        [shape(8, 128, dtype=jnp.int32), shape(rows_p, 128), level, level, shape(2 * wide, 128), message],
    )
    low, high, sums = low0, high0, []
    scratch = [pltpu.VMEM((2, NF, wide, rows_t), f32) for _ in range(3)]
    for stage in range(1, 5):
        below = exchanged(low, "rad", 0)
        above = exchanged(high, "rad", 1)
        ins = [sines, low0, high0, below, above, crossed(answer), table]
        if stage > 1:
            ins += [low, high, *sums]
        if stage < 4:
            ins += [lanes, rowmask]
            outs = [level, level, own_level, own_level, message]
        else:
            outs = [
                shape(1, rows_r, rows_p, rows_t, final=True),
                shape(1, 3, rows_r, rows_p, rows_t, final=True),
                shape(1, 3, rows_r, rows_p, rows_t, final=True),
            ]

        def kernel(*refs, stage=stage):
            stage_kernel(stage, n_rad, n_ang, *refs)

        result = call(kernel, ins, outs, scratch)
        if stage == 4:
            return tuple(result)
        low, high, acc_low, acc_high, answer = result
        sums = [acc_low, acc_high]


def solution(mesh):
    in_specs = (
        P("panel", "rad", "ang", None),
        P("panel", None, "rad", "ang", None),
        P("panel", None, "rad", "ang", None),
        P("panel", "ang", None),
        P("panel", "ang"),
        P("panel", "ang"),
        P("panel", "ang", None),
        P("panel", "ang"),
    )
    out_specs = (
        P("panel", "rad", "ang", None),
        P("panel", None, "rad", "ang", None),
        P("panel", None, "rad", "ang", None),
    )
    return jax.shard_map(body, mesh=mesh, in_specs=in_specs, out_specs=out_specs, check_vma=False)
```

```python
import math

import jax
import jax.numpy as jnp
import numpy as np
from jax import lax
from jax.experimental import pallas as pl
from jax.experimental.pallas import tpu as pltpu
from jax.sharding import PartitionSpec as P

time_step = 0.15
diffusion = 0.1
r_inner = 0.35
NF = 7
MIRROR = (1.0, -1.0, -1.0, -1.0, 1.0, 1.0, 1.0)
INTERPRET = False
EDGE = 4
SLOT = 16
HIGHEST = lax.Precision.HIGHEST


def iota(shape, dim):
    return lax.broadcasted_iota(jnp.int32, shape, dim)


def derived(cells):
    inverse = 1.0 / cells[0]
    speed = [cells[1 + c] * inverse for c in range(3)]
    pressure = cells[0] + 0.5 * (
        cells[4] * cells[4] + cells[5] * cells[5] + cells[6] * cells[6]
    )
    return speed, pressure


def stresses(cells, speed, pressure, pairs):
    moment, magnet = cells[1:4], cells[4:7]
    out = {}
    for c, d in pairs:
        term = moment[c] * speed[d] - magnet[c] * magnet[d]
        if c == d:
            out["T", c, d] = term + pressure
        else:
            out["T", c, d] = out["T", d, c] = term
            out["E", c, d] = speed[c] * magnet[d] - magnet[c] * speed[d]
    return out


def flux_along(cells, found, d):
    out = [(1, cells[1 + d])]
    for c in range(3):
        out.append((1, found["T", d, c]))
    for c in range(3):
        if c == d:
            out.append((0, None))
        elif c > d:
            out.append((1, found["E", d, c]))
        else:
            out.append((-1, found["E", c, d]))
    return out


ALL_PAIRS = ((0, 0), (0, 1), (0, 2), (1, 1), (1, 2), (2, 2))


def given(flux, cell, half, spread):
    sign, value = flux
    if cell is None:
        moved = half * value
        return moved, -moved
    spreading = spread * cell
    if not sign:
        return spreading, spreading
    moved = half * value
    plus, minus = spreading + moved, spreading - moved
    return (plus, minus) if sign > 0 else (minus, plus)


def inverse_radius(rad, n_rad, slot, rows_r):
    value = None
    for at in range(n_rad):
        level = 1 - (at & 1) if slot == 0 else at & 1
        radius = r_inner + (at * rows_r + level + 0.5) * ((1.0 - r_inner) / (rows_r * n_rad))
        item = jnp.float32(1.0 / radius)
        value = item if value is None else jnp.where(rad == at, item, value)
    return value


def partners(size, step):
    return [(i, (i ^ 1) if step == 0 else (((i + 1) ^ 1) - 1) % size) for i in range(size)]


def answer_part(cells, lanes, rowmask):
    at, tile = lanes & 127, lanes >> 7
    out = []
    for field in cells:
        total = None
        for row in range(0, rowmask.shape[0], 8):
            found = None
            for q in range(field.shape[1] // 128):
                item = jnp.take_along_axis(
                    field[row : row + 8, 128 * q : 128 * q + 128], at, axis=1, mode="promise_in_bounds"
                )
                found = item if found is None else jnp.where(tile == q, item, found)
            found = found * rowmask[row : row + 8, :]
            total = found if total is None else total + found
        out.append(jnp.sum(total, axis=0, keepdims=True))
    return out


def answer_into(msg_ref, picked):
    gap = jnp.zeros((1, 128), jnp.float32)
    parts = [*picked[0], gap, *picked[1], gap]
    both = jnp.concatenate(parts, axis=0)
    both = both + pltpu.roll(both, 64, axis=1)
    turned = both.T
    turned = jnp.concatenate([turned, jnp.zeros((128, 128 - SLOT), jnp.float32)], axis=1)
    own = turned[0:32] + pltpu.roll(turned[32:64], SLOT, axis=1)
    before = pltpu.roll(pltpu.roll(own, 1, axis=0), 2 * SLOT, axis=1)
    after = pltpu.roll(pltpu.roll(own, 31, axis=0), 4 * SLOT, axis=1)
    msg_ref[...] = (own + before + after).reshape(msg_ref.shape)


def open_kernel(
    density, momentum, magnetic, device, phi, theta, weight, turn, sines,
    low_ref, high_ref, first_ref, last_ref, ask_ref, table_ref, sines_ref,
):
    sines_ref[...] = sines[...]
    odd = lax.axis_index("rad") & 1
    even_ang = (lax.axis_index("ang") & 1) == 0

    def edges(f, at, top, bottom):
        width = top.shape[1]
        first_ref[f, at : at + EDGE, 0:width] = jnp.where(even_ang, bottom, top)
        last_ref[f, at : at + EDGE, 0:width] = jnp.where(even_ang, top, bottom)

    for slot, ref in ((0, low_ref), (1, high_ref)):
        level = 1 - odd if slot == 0 else odd
        for f in range(NF):
            if f == 0:
                value = density[0, level]
            elif f < 4:
                value = momentum[0, f - 1, level]
            else:
                value = magnetic[0, f - 4, level]
            ref[f] = value
            edges(f, EDGE * slot, value[:EDGE], value[value.shape[0] - EDGE :])
    rows = device.shape[2]
    one, two = iota((rows, rows), 0), iota((rows, rows), 1)
    eye = one == two
    dev_row = device[0]
    dev_col = jnp.sum(jnp.where(eye, jnp.broadcast_to(dev_row, (rows, rows)), 0), axis=1, keepdims=True)
    same = dev_col == dev_row
    rank_row = jnp.sum(jnp.where(same & (one < two), 1, 0), axis=0, keepdims=True)
    rank_col = jnp.sum(jnp.where(same & (two < one), 1, 0), axis=1, keepdims=True)

    def column(row):
        return jnp.sum(jnp.where(eye, jnp.broadcast_to(row, (rows, rows)), 0.0), axis=1, keepdims=True)

    phi_col = column(phi[...].astype(jnp.float32))
    theta_col = column(theta[...].astype(jnp.float32))
    weights = weight[0]
    lane = iota((rows, 128), 1)
    items = [phi_col, theta_col] + [column(weights[c : c + 1, :]) for c in range(4)]
    record = jnp.zeros((rows, 128), jnp.float32)
    for at, item in enumerate(items):
        record = jnp.where(lane == at, item, record)
    asked = jnp.zeros((rows, 128), jnp.float32)
    for slot in range(2):
        placing = jnp.where((one == dev_row) & (rank_row == slot), 1.0, 0.0)
        moved = record if slot == 0 else pltpu.roll(record, 8, axis=1)
        asked = asked + jnp.dot(placing, moved, precision=HIGHEST, preferred_element_type=jnp.float32)
    ask_ref[...] = asked.reshape(ask_ref.shape)
    picks = jnp.where(((lane & 31) == dev_col) & ((lane >> 5) == rank_col) & (lane < 64), 1.0, 0.0)
    cosine = column(jnp.cos(turn[...]))
    sine = column(jnp.sin(turn[...]))
    picks = jnp.where(lane == 64, cosine, picks)
    picks = jnp.where(lane == 65, sine, picks)
    table_ref[...] = picks
    half = rows // 2
    for side in range(2):
        at = half * side
        edges(NF, EDGE * side, picks[at : at + EDGE], picks[at + half - EDGE : at + half])
    for ref in (first_ref, last_ref):
        ref[NF, :, 128:] = jnp.zeros((2 * EDGE, ref.shape[2] - 128), jnp.float32)


def asked_kernel(
    asked_ref, low_ref, high_ref, one_ref, two_ref, table_ref,
    lanes_ref, mask_ref, low_out, high_out, table_out, msg_ref,
):
    own_rows = low_ref.shape[1]
    even_ang = (lax.axis_index("ang") & 1) == 0

    def beside(f, rows, width):
        one, two = one_ref[f, rows, 0:width], two_ref[f, rows, 0:width]
        return jnp.where(even_ang, two, one), jnp.where(even_ang, one, two)

    for level, ref, out in ((0, low_ref, low_out), (1, high_ref, high_out)):
        rows = slice(EDGE * level, EDGE * level + EDGE)
        for f in range(NF):
            before, after = beside(f, rows, ref.shape[2])
            out[f] = jnp.concatenate([ref[f], after, before], axis=0)
    pieces = []
    for side in range(2):
        rows = slice(EDGE * side, EDGE * side + EDGE)
        half = own_rows * side
        before, after = beside(NF, rows, 128)
        pieces += [table_ref[half : half + own_rows, :], after, before]
    table_out[...] = jnp.concatenate(pieces, axis=0)
    asked = asked_ref[...].reshape(32, 128)
    lane, sub = iota((32, 128), 1), iota((32, 128), 0)

    def row_of(at):
        total = jnp.zeros((32, 128), jnp.float32)
        for part in range(4):
            slot = part & 1
            col = asked[:, slot * 8 + at[part >> 1] : slot * 8 + at[part >> 1] + 1]
            total = jnp.where(lane == sub + 32 * part, col, total)
        return jnp.sum(total, axis=0, keepdims=True)

    phi_row = row_of((0, 0)).astype(jnp.int32)
    theta_row = row_of((1, 1)).astype(jnp.int32) + jnp.where(iota((1, 128), 1) < 64, 0, 1)
    near = row_of((2, 3))
    far = row_of((4, 5))
    lanes = jnp.broadcast_to(theta_row, (8, 128))
    lanes_ref[...] = lanes
    rows_p = mask_ref.shape[0]
    at = iota((rows_p, 128), 0)
    mask = jnp.where(at == phi_row, near, jnp.where(at == phi_row + 1, far, 0.0))
    mask_ref[...] = mask
    answer_into(
        msg_ref,
        [answer_part([ref[f] for f in range(NF)], lanes, mask) for ref in (low_ref, high_ref)],
    )


def ghosts_of(reply, table):
    got = reply[...].reshape(32, 128)
    picks = table[...]
    rows = picks.shape[0]
    half = rows // 2
    ghost = jnp.dot(picks[:, 0:32], got, precision=HIGHEST, preferred_element_type=jnp.float32)
    second = jnp.dot(picks[:, 32:64], got, precision=HIGHEST, preferred_element_type=jnp.float32)
    ghost = ghost + pltpu.roll(second, 128 - SLOT, axis=1)
    row = iota((rows, 128), 0)
    row = jnp.where(row < half, row, row - half)
    before = pltpu.roll(ghost, 128 - 2 * SLOT, axis=1)
    after = pltpu.roll(ghost, 128 - 4 * SLOT, axis=1)
    ghost = jnp.where(row < half - 2 * EDGE, ghost, jnp.where(row < half - EDGE, after, before))
    cosine, sine = picks[:, 64:65], picks[:, 65:66]
    lane = iota((rows, 128), 1) & 7
    is_t = (lane == 2) | (lane == 5)
    is_p = (lane == 3) | (lane == 6)
    turned_t = cosine * ghost + sine * pltpu.roll(ghost, 127, axis=1)
    turned_p = cosine * ghost - sine * pltpu.roll(ghost, 1, axis=1)
    return jnp.where(is_t, turned_t, jnp.where(is_p, turned_p, ghost))


def stage_kernel(stage, n_rad, n_ang, *refs):
    last = stage == 4
    (sines, low0, high0, below, above, reply, table) = refs[:7]
    refs = refs[7:]
    if stage == 1:
        low, high = low0, high0
    else:
        low, high = refs[:2]
        refs = refs[2:]
    if last:
        two, three = refs[0:2], refs[2:4]
        density_out, momentum_out, magnetic_out = refs[4:7]
        refs = refs[7:]
    else:
        lanes, rowmask = refs[:2]
        low_out, high_out, msg_out = refs[2:5]
        refs = refs[5:]
    slope, up, down = refs
    rad, ang = lax.axis_index("rad"), lax.axis_index("ang")
    rows_p, rows_t = low.shape[1:]
    width = rows_t + 128
    invs = [inverse_radius(rad, n_rad, slot, 2) for slot in range(2)]
    outward = jnp.where((rad & 1) == 0, jnp.float32(0.5), jnp.float32(-0.5))
    wall = (rad == 0) | (rad == n_rad - 1)
    ghost = ghosts_of(reply, table)
    sine_row = sines[...]
    own = rows_p - 2 * EDGE
    half_row = iota((8, 128), 1) < 64
    r_pairs = ((0, 0), (0, 1), (0, 2))
    t_pairs = ((0, 1), (1, 1), (1, 2))
    p_pairs = ((0, 2), (1, 2), (2, 2))
    for tile in range(rows_p // 8):
        rows = slice(8 * tile, 8 * tile + 8)
        both = [[ref[f, rows, :] for f in range(NF)] for ref in (low, high)]
        if last and 8 * tile >= own:
            for slot in range(2):
                cells = both[slot]
                inv_sine = invs[slot] * sine_row
                half, spread = 0.5 * inv_sine, diffusion * inv_sine * inv_sine
                p_flux = flux_along(cells, stresses(cells, *derived(cells), p_pairs), 2)
                for f in range(NF):
                    cell = cells[f] if f else None
                    down[slot, f, rows, :], up[slot, f, rows, :] = given(p_flux[f], cell, half, spread)
            continue
        found, r_flux = [], []
        for cells in both:
            found.append(stresses(cells, *derived(cells), ALL_PAIRS))
            r_flux.append(flux_along(cells, found[-1], 0))
        for slot in range(2):
            cells, inner, inner_flux = both[slot], both[1 - slot], r_flux[1 - slot]
            outer = [(below if slot == 0 else above)[f, rows, :] for f in range(NF)]
            if slot == 1:
                outer = [jnp.where(wall, MIRROR[f] * cells[f], outer[f]) for f in range(NF)]
            outer_flux = flux_along(outer, stresses(outer, *derived(outer), r_pairs), 0)
            half_r = outward if slot == 0 else -outward
            inv = invs[slot]
            inv_sine = inv * sine_row
            half, spread = 0.5 * inv_sine, diffusion * inv_sine * inv_sine
            half_t, spread_t = 0.5 * inv, diffusion * inv * inv
            centre = 2.0 * diffusion + 2.0 * spread_t + 2.0 * spread
            rim = []
            for f in range(NF):
                at = 8 * slot + f
                lower = ghost[8 * tile : 8 * tile + 8, at : at + 1]
                upper = ghost[rows_p + 8 * tile : rows_p + 8 * tile + 8, at : at + 1]
                rim.append(jnp.where(half_row, upper, lower))
            rim_flux = flux_along(rim, stresses(rim, *derived(rim), t_pairs), 1)
            t_flux = flux_along(cells, found[slot], 1)
            p_flux = flux_along(cells, found[slot], 2)
            for f in range(NF):
                cell = cells[f] if f else None
                down[slot, f, rows, :], up[slot, f, rows, :] = given(p_flux[f], cell, half, spread)
                total = None
                if r_flux[slot][f][0]:
                    total = half_r * (inner_flux[f][1] - outer_flux[f][1])
                if f:
                    item = diffusion * (inner[f] + outer[f]) - centre * cell
                    total = item if total is None else total + item
                whole = (t_flux[f][0], None)
                if t_flux[f][0]:
                    whole = (t_flux[f][0], jnp.concatenate([t_flux[f][1], rim_flux[f][1]], axis=1))
                full = jnp.concatenate([cell, rim[f]], axis=1) if f else None
                to_upper, to_lower = given(whole, full, half_t, spread_t)
                total = total + pltpu.roll(to_upper, 1, axis=1)[:, :rows_t]
                slope[slot, f, rows, :] = total + pltpu.roll(to_lower, width - 1, axis=1)[:, :rows_t]

    @pl.when(ang == 0)
    def _():
        for slot in range(2):
            for f in range(NF):
                down[slot, f, rows_p - 1 :, :] = MIRROR[f] * up[slot, f, 0:1, :]

    @pl.when(ang == n_ang - 1)
    def _():
        for slot in range(2):
            for f in range(NF):
                up[slot, f, own : own + 1, :] = MIRROR[f] * down[slot, f, own - 1 : own, :]

    picked = []
    used = own if last else rows_p
    for slot in range(2):
        start = low0 if slot == 0 else high0
        values = []
        for f in range(NF):
            k = slope[slot, f, :used] + pltpu.roll(down[slot, f], 1, axis=0)[:used]
            k = k + pltpu.roll(up[slot, f], rows_p - 1, axis=0)[:used]
            if last:
                level = 1 - (rad & 1) if slot == 0 else rad & 1
                now = low if slot == 0 else high
                value = two[slot][f, :own] + 2.0 * three[slot][f, :own] + now[f, :own] - start[f, :own]
                value = (1.0 / 3.0) * value + (time_step / 6.0) * k
                if f == 0:
                    density_out[0, level] = value
                elif f < 4:
                    momentum_out[0, f - 1, level] = value
                else:
                    magnetic_out[0, f - 4, level] = value
                continue
            step = time_step if stage == 3 else 0.5 * time_step
            value = start[f] + step * k
            (low_out if slot == 0 else high_out)[f] = value
            values.append(value[:own])
        if not last:
            picked.append(answer_part(values, lanes[...], rowmask[...]))
    if not last:
        answer_into(msg_out, picked)


def body(
    density, momentum, magnetic, partner_device, partner_phi, partner_theta, partner_weight, border_turn
):
    _, rows_r, rows_p, rows_t = density.shape
    n_ang, n_rad = lax.axis_size("ang"), lax.axis_size("rad")
    f32 = jnp.float32
    vmem = pl.BlockSpec(memory_space=pltpu.VMEM)

    def shape(*dims, final=False, dtype=f32):
        return jax.ShapeDtypeStruct(dims, dtype) if final or INTERPRET else pltpu.VMEM(dims, dtype)

    def held(value):
        return value if INTERPRET else pltpu.with_memory_space_constraint(value, pltpu.VMEM)

    def call(kernel, ins, outs, scratch=(), plain=0):
        return pl.pallas_call(
            kernel,
            out_shape=outs,
            in_specs=[vmem] * len(ins),
            out_specs=[vmem] * len(outs),
            scratch_shapes=list(scratch),
            interpret=INTERPRET,
            compiler_params=pltpu.CompilerParams(vmem_limit_bytes=None if plain > 1 else 12 << 20),
        )(*[item if at < plain else held(item) for at, item in enumerate(ins)])

    wide = rows_p + 2 * EDGE
    own_level = shape(NF, rows_p, rows_t)
    level = shape(NF, wide, rows_t)
    edge = shape(NF + 1, 2 * EDGE, rows_t)
    message = shape(32, 1, 128)

    def exchanged(value, axis, step):
        return held(lax.ppermute(value, axis, partners(lax.axis_size(axis), step)))

    def crossed(value):
        swap = held(lax.ppermute(value, "panel", [(0, 1), (1, 0)]))
        return held(lax.all_to_all(swap, "ang", split_axis=0, concat_axis=0, tiled=True))

    theta = math.pi / 4 + (np.arange(rows_t) + 0.5) * (math.pi / 2 / rows_t)
    sines = jnp.asarray((1.0 / np.sin(theta)).astype(np.float32)).reshape(1, rows_t)

    low0, high0, first, final, ask, table, sines = call(
        open_kernel,
        [
            density, momentum, magnetic, jnp.swapaxes(partner_device, 1, 2), partner_phi, partner_theta,
            jnp.swapaxes(partner_weight, 1, 2), border_turn, sines,
        ],
        [own_level, own_level, edge, edge, message, shape(32, 128), shape(1, rows_t)],
        plain=9,
    )
    one = exchanged(first, "ang", 0)
    two = exchanged(final, "ang", 1)
    lanes, rowmask, low0, high0, table, answer = call(
        asked_kernel,
        [crossed(ask), low0, high0, one, two, table],
        [shape(8, 128, dtype=jnp.int32), shape(rows_p, 128), level, level, shape(2 * wide, 128), message],
    )
    low, high, kept = low0, high0, []
    scratch = [pltpu.VMEM((2, NF, wide, rows_t), f32) for _ in range(3)]
    for stage in range(1, 5):
        below = exchanged(low, "rad", 0)
        above = exchanged(high, "rad", 1)
        ins = [sines, low0, high0, below, above, crossed(answer), table]
        if stage > 1:
            ins += [low, high]
        if stage < 4:
            ins += [lanes, rowmask]
            outs = [level, level, message]
        else:
            ins += kept
            outs = [
                shape(1, rows_r, rows_p, rows_t, final=True),
                shape(1, 3, rows_r, rows_p, rows_t, final=True),
                shape(1, 3, rows_r, rows_p, rows_t, final=True),
            ]

        def kernel(*refs, stage=stage):
            stage_kernel(stage, n_rad, n_ang, *refs)

        result = call(kernel, ins, outs, scratch)
        if stage == 4:
            return tuple(result)
        low, high, answer = result
        if stage < 3:
            kept += [low, high]


def solution(mesh):
    in_specs = (
        P("panel", "rad", "ang", None),
        P("panel", None, "rad", "ang", None),
        P("panel", None, "rad", "ang", None),
        P("panel", "ang", None),
        P("panel", "ang"),
        P("panel", "ang"),
        P("panel", "ang", None),
        P("panel", "ang"),
    )
    out_specs = (
        P("panel", "rad", "ang", None),
        P("panel", None, "rad", "ang", None),
        P("panel", None, "rad", "ang", None),
    )
    return jax.shard_map(body, mesh=mesh, in_specs=in_specs, out_specs=out_specs, check_vma=False)
```
